128 devices in a mesh: gr: 16 (over y_hi, z, core), gc: 8 (over x, y_lo).
Axes of the slice: x: 4, y: 4 (y_hi: 2, y_lo: 2; y = y_hi * 2 + y_lo), z: 4, core: 2. Of those that a mesh axis runs over, the one named last changes fastest.
Arguments:
- shards: bfloat16 [16, 8, 56, 18432], P('gr', 'gc'), may hold values from -4.5 to 4.5, as said below
- counts: int32 [8, 16], replicated, may hold values from 1 to 56, 448 in all within a row
Outputs:
- next_shards: float32 [16, 8, 56, 18432], P('gr', 'gc')
The draws below stay inside these ranges and needn't reach their ends.
Inputs may be any that keep to these rules, and one draw needn't show every extreme that they name: Each row of counts sums to 448: the devices (0, c) to (15, c) together hold row block c of the iterate, in order of g. `shards`: rows of a buffer at or beyond its device's count are not part of the iterate and hold arbitrary values.
All inputs are finite; a program needn't handle non-finite values.
Results may differ from the reference program's by a relative error of at most 0.0003.
Values may be sent and summed in bfloat16 or wider, within the bound.
A program may use at most 128 MiB of HBM per device.

```python
import math
import jax
import jax.numpy as jnp
import numpy as np
from jax import lax

M = 3584
N = 18432
RB = 448
CAP = 56
N_GR = 16
N_GC = 8


def draw_shards(key, part):
    array_shape = (N_GR, N_GC, CAP, N)
    values = 0.75 * jax.random.truncated_normal(key, -6.0, 6.0, array_shape, jnp.float32)
    return values.astype(jnp.bfloat16)


def split_up(amount, total, reach, lean):
    loads = [(1 << 20) // math.isqrt(grade ** lean) + 1 for grade in range(2, amount + 1)]
    spare, given = total - reach - (amount - 1), [1] * (amount - 1)
    while spare > 0:
        candidates = [i for i in range(amount - 1) if given[i] < reach]
        pool, left = sum([loads[i] for i in candidates]), spare
        for i in candidates:
            more = min(reach - given[i], max(1, left * loads[i] // pool), spare)
            given[i] = given[i] + more
            spare = spare - more
    return np.array([reach] + given)


def uneven_parts(stream_key, count, total, bound, lean):
    if count == 2:
        one = jax.random.randint(stream_key, (), max(1, total - bound), min(bound, total - 1) + 1)
        return jnp.stack([one, total - one])
    lengths = jnp.asarray(split_up(count, total, bound, lean), jnp.int32)
    pairs = (count - 1) // 2
    donor, taker = lengths[1:1 + 2 * pairs:2], lengths[2:2 + 2 * pairs:2]
    room = jnp.minimum(donor - 1, bound - taker)
    moved = jax.random.randint(jax.random.fold_in(stream_key, 1), (pairs,), 0, 1 << 20) % (room + 1)
    lengths = lengths.at[1:1 + 2 * pairs:2].set(donor - moved).at[2:2 + 2 * pairs:2].set(taker + moved)
    return lengths[jax.random.permutation(jax.random.fold_in(stream_key, 2), count)]


def setup_inputs(seed: int = 0) -> dict:
    splits = jax.random.split(jax.random.key(seed), 3)
    shards = draw_shards(jax.random.fold_in(splits[2], 71), 0)
    counts = jax.vmap(lambda own: uneven_parts(own, N_GR, RB, CAP, 2))(jax.random.split(splits[1], N_GC)).reshape((N_GC, N_GR)).astype(jnp.int32)
    return dict(shards=shards, counts=counts)


linear_coef = 3.4445
cubic_coef = -4.7750
quintic_coef = 2.0315


def reference(shards, counts):
    starts = (jnp.cumsum(counts, axis=1) - counts).astype(jnp.int32)
    within_block = jnp.arange(RB, dtype=jnp.int32)
    holder = (jnp.sum((starts[:, None, :] <= within_block[None, :, None]).astype(jnp.int32), axis=2) - 1).astype(jnp.int32)
    first_row = jnp.take_along_axis(starts, holder, axis=1).astype(jnp.int32)
    within = (within_block[None, :] - first_row).astype(jnp.int32)
    block_ids = (jnp.arange(N_GC, dtype=jnp.int32)[:, None] + jnp.zeros_like(holder)).astype(jnp.int32)
    iterate = shards[holder, block_ids, within].reshape(M, N)
    gram_matrix = jnp.dot(iterate, iterate.T, preferred_element_type=jnp.float32) / N
    square = jnp.dot(gram_matrix, gram_matrix, precision=lax.Precision.HIGHEST, preferred_element_type=jnp.float32)
    polynomial = cubic_coef * gram_matrix + quintic_coef * square
    widened = iterate.astype(jnp.float32)
    update = linear_coef * widened + jnp.dot(polynomial, widened, precision=lax.Precision.HIGHEST, preferred_element_type=jnp.float32)
    slot_ids = jnp.arange(CAP, dtype=jnp.int32)
    base_rows = (jnp.arange(N_GC, dtype=jnp.int32)[None, :] * RB + starts.T).astype(jnp.int32)
    row_index = jnp.minimum(base_rows[:, :, None] + slot_ids[None, None, :], M - 1).astype(jnp.int32)
    is_valid = slot_ids[None, None, :] < counts.T[:, :, None]
    return jnp.where(is_valid[..., None], update[row_index], jnp.zeros((), jnp.float32))
```

```python
import jax
import jax.numpy as jnp
from jax import lax
from jax.experimental import pallas as pl
from jax.experimental.pallas import tpu as pltpu
from jax.sharding import PartitionSpec as P

M = 3584
N = 18432
CAP = 56
RB = 448
WIDTH = 1152
PIECE_ROWS = 112
PIECE_COLS = 896

linear_coef = 3.4445
cubic_coef = -4.775
quintic_coef = 2.0315

MESH = pl.DeviceIdType.MESH
f32 = jnp.float32
bf16 = jnp.bfloat16


def mod(value, size):
    return lax.rem(value, jnp.int32(size))


def position():
    gr = lax.axis_index("gr")
    gc = lax.axis_index("gc")
    half = lax.div(gr, jnp.int32(2))
    x = lax.div(gc, jnp.int32(2))
    y = lax.div(half, jnp.int32(4)) * 2 + mod(gc, 2)
    return x, y, mod(half, 4), mod(gr, 2)


def device(x, y, z, core):
    return {
        "gr": (lax.div(y, jnp.int32(2)) * 4 + z) * 2 + core,
        "gc": x * 2 + mod(y, 2),
    }


def greet(x, y, z, core):
    barrier = pltpu.get_barrier_semaphore()
    count = 0
    for dy in range(4):
        for dz in range(4):
            for dc in range(2):
                if dy or dz or dc:
                    target = device(x, mod(y + dy, 4), mod(z + dz, 4), mod(core + dc, 2))
                    pl.semaphore_signal(barrier, inc=1, device_id=target, device_id_type=MESH)
                    count += 1
    for dx in (1, 3):
        target = device(mod(x + dx, 4), y, z, core)
        pl.semaphore_signal(barrier, inc=1, device_id=target, device_id_type=MESH)
        count += 1
    pl.semaphore_wait(barrier, count)


class Courier:
    def __init__(self, send_sem, recv_sem):
        self.send_sem, self.recv_sem = send_sem, recv_sem
        self.copies = []

    def send(self, src, dst, target):
        index = len(self.copies)
        copy = pltpu.make_async_remote_copy(
            src_ref=src,
            dst_ref=dst,
            send_sem=self.send_sem.at[index],
            recv_sem=self.recv_sem.at[index],
            device_id=target,
            device_id_type=MESH,
        )
        self.copies.append(copy)
        copy.start()
        return copy

    def drain(self):
        for copy in self.copies:
            copy.wait_send()


class RingGather:
    def __init__(self, courier, part_a, part_b, pos, right, left):
        self.courier, self.part_a, self.part_b = courier, part_a, part_b
        self.pos, self.right, self.left = pos, right, left
        a, b = part_a(pos), part_b(pos)
        self.a_right = courier.send(a, a, right)
        self.b_left = courier.send(b, b, left)
        self.b_right = courier.send(b, b, right)
        self.a_left = courier.send(a, a, left)

    def relay(self):
        self.a_right.wait_recv()
        a = self.part_a(mod(self.pos + 3, 4))
        self.a_far = self.courier.send(a, a, self.right)
        self.b_left.wait_recv()
        b = self.part_b(mod(self.pos + 1, 4))
        self.b_far = self.courier.send(b, b, self.left)

    def near(self):
        self.b_right.wait_recv()
        self.a_left.wait_recv()

    def far(self):
        self.a_far.wait_recv()
        self.b_far.wait_recv()


class RingReduce:
    def __init__(self, courier, part_a, part_b, bufs, cut, pos, right, left):
        self.courier, self.part_a, self.part_b = courier, part_a, part_b
        self.pos, self.right, self.left = pos, right, left
        self.tmp_a, self.tmp_b, self.from_left, self.from_right = bufs
        self.in_a, self.in_b = cut
        far = mod(pos + 2, 4)
        self.a1 = courier.send(part_a(far), self.tmp_a, right)
        self.b1 = courier.send(part_b(far), self.tmp_b, left)
        self.a2 = courier.send(part_b(mod(pos + 1, 4)), self.in_b(self.from_left), right)
        self.b2 = courier.send(part_a(mod(pos + 3, 4)), self.in_a(self.from_right), left)

    def relay(self):
        self.a1.wait_recv()
        a = self.part_a(mod(self.pos + 1, 4))
        a[...] = a[...] + self.tmp_a[...]
        self.a3 = self.courier.send(a, self.in_a(self.from_left), self.right)
        self.b1.wait_recv()
        b = self.part_b(mod(self.pos + 3, 4))
        b[...] = b[...] + self.tmp_b[...]
        self.b3 = self.courier.send(b, self.in_b(self.from_right), self.left)

    def finish(self):
        for copy in (self.a2, self.b2, self.a3, self.b3):
            copy.wait_recv()


def gram_kernel(
    shard, target_rows, panel, gram_piece, received, wide, part,
    big_tmp, big_recv, small_tmp_a, small_tmp_b, small_recv,
    send_sem, recv_sem, in_send, in_recv,
):
    x, y, z, core = position()
    greet(x, y, z, core)
    y_lo = mod(y, 2)
    me = lax.axis_index("gr")
    at_home = core == y_lo

    def columns(dy, dz):
        block = mod(y + dy, 4) * 4 + mod(z + dz, 4)
        return shard.at[:, pl.ds(pl.multiple_of(block * WIDTH, 128), WIDTH)]

    def outward(index, dy, dz):
        return pltpu.make_async_remote_copy(
            src_ref=columns(dy, dz),
            dst_ref=received.at[me],
            send_sem=in_send.at[index],
            recv_sem=in_recv.at[me],
            device_id=device(x, mod(y + dy, 4), mod(z + dz, 4), y_lo),
            device_id_type=MESH,
        )

    offsets = [(dy, dz) for dy in range(4) for dz in range(4)]
    offsets = sorted(offsets, key=lambda o: -(min(o[0], 4 - o[0]) + min(o[1], 4 - o[1])))
    for index, (dy, dz) in enumerate(offsets):
        if dy or dz:
            outward(index, dy, dz).start()
        else:
            @pl.when(at_home)
            def _():
                pltpu.make_async_copy(columns(0, 0), received.at[me], in_recv.at[me]).start()

            @pl.when(jnp.logical_not(at_home))
            def _():
                outward(index, 0, 0).start()
    for g in range(16):
        pltpu.make_async_copy(received.at[g], received.at[g], in_recv.at[g]).wait()
        wide[g * CAP:(g + 1) * CAP] = received[g].astype(f32)

    rows = lax.broadcasted_iota(jnp.int32, (RB, 16 * CAP), 0)
    pick = (rows == target_rows[...]).astype(f32).astype(bf16)
    own = panel.at[x, pl.ds(pl.multiple_of(core * RB, RB), RB)]
    for low, size in ((0, 512), (512, 640)):
        own[:, low:low + size] = jnp.dot(
            pick, wide[:, low:low + size].astype(bf16), preferred_element_type=f32
        ).astype(bf16)

    courier = Courier(send_sem, recv_sem)
    partner = device(x, y, z, 1 - core)

    def slot(low):
        def part_of(pos):
            return panel.at[pos, pl.ds(pl.multiple_of(core * RB + low, 32), RB // 2)]
        return part_of

    def whole(pos):
        return panel.at[pos, pl.ds(pl.multiple_of(core * RB, 32), RB)]

    ring = RingGather(
        courier, slot(0), slot(RB // 2), x,
        device(mod(x + 1, 4), y, z, core), device(mod(x + 3, 4), y, z, core),
    )
    across = [courier.send(whole(x), whole(x), partner)]

    def multiply(pos):
        product = lax.dot_general(
            own[...], panel[pos], (((1,), (1,)), ((), ())), preferred_element_type=f32
        )
        part[pos] = (product * (1.0 / N)).reshape(4, 2, CAP, PIECE_COLS)

    ring.relay()
    ring.near()
    for step in (1, 3):
        pos = mod(x + step, 4)
        across.append(courier.send(whole(pos), whole(pos), partner))
    across[0].wait_recv()
    multiply(x)
    across[1].wait_recv()
    multiply(mod(x + 1, 4))
    across[2].wait_recv()
    multiply(mod(x + 3, 4))
    ring.far()
    pos = mod(x + 2, 4)
    across.append(courier.send(whole(pos), whole(pos), partner))
    across[3].wait_recv()
    multiply(pos)

    z_right, z_left = device(x, y, mod(z + 1, 4), core), device(x, y, mod(z + 3, 4), core)
    y_right, y_left = device(x, mod(y + 1, 4), z, core), device(x, mod(y + 3, 4), z, core)
    first, second = (lambda r: r.at[0:2]), (lambda r: r.at[2:4])
    upper, lower = (lambda r: r.at[0:32]), (lambda r: r.at[32:CAP])

    def bufs(tmp_a, tmp_b, recv, half):
        return tmp_a.at[half], tmp_b.at[half], recv.at[half, 0], recv.at[half, 1]

    big = lambda half: bufs(big_tmp.at[0], big_tmp.at[1], big_recv, half)
    small = lambda half: bufs(small_tmp_a, small_tmp_b, small_recv, half)
    one = RingReduce(
        courier, lambda p: part.at[0:2, p, 0], lambda p: part.at[2:4, p, 0],
        big(0), (first, second), z, z_right, z_left,
    )
    two = RingReduce(
        courier, lambda p: part.at[p, 0:2, 1], lambda p: part.at[p, 2:4, 1],
        big(1), (first, second), y, y_right, y_left,
    )
    one.relay()
    two.relay()
    one.finish()
    part[:, z, 0] = part[:, z, 0] + big_recv[0, 0] + big_recv[0, 1]
    three = RingReduce(
        courier, lambda p: upper(part.at[p, z, 0]), lambda p: lower(part.at[p, z, 0]),
        small(0), (upper, lower), y, y_right, y_left,
    )
    two.finish()
    part[y, :, 1] = part[y, :, 1] + big_recv[1, 0] + big_recv[1, 1]
    four = RingReduce(
        courier, lambda p: upper(part.at[y, p, 1]), lambda p: lower(part.at[y, p, 1]),
        small(1), (upper, lower), z, z_right, z_left,
    )
    three.relay()
    four.relay()
    three.finish()
    gram_piece[0:CAP] = part[y, z, 0] + small_recv[0, 0] + small_recv[0, 1]
    four.finish()
    gram_piece[CAP:2 * CAP] = part[y, z, 1] + small_recv[1, 0] + small_recv[1, 1]
    courier.drain()
    for index, (dy, dz) in enumerate(offsets):
        if dy or dz:
            outward(index, dy, dz).wait_send()
        else:
            @pl.when(jnp.logical_not(at_home))
            def _():
                outward(index, 0, 0).wait_send()


def split(value):
    high = value.astype(bf16)
    return high, (value - high.astype(f32)).astype(bf16)


def update_kernel(
    slot_rows, gram_piece, panel, result, gram_cols, gram_rows, square, poly,
    pick, outgoing, send_sem, recv_sem, out_send, out_recv,
):
    x, y, z, core = position()
    greet(x, y, z, core)
    courier = Courier(send_sem, recv_sem)
    partner = device(x, y, z, 1 - core)
    z_right, z_left = device(x, y, mod(z + 1, 4), core), device(x, y, mod(z + 3, 4), core)
    y_right, y_left = device(x, mod(y + 1, 4), z, core), device(x, mod(y + 3, 4), z, core)
    x_right, x_left = device(mod(x + 1, 4), y, z, core), device(mod(x + 3, 4), y, z, core)

    for h, value in enumerate(split(gram_piece[...])):
        gram_cols[h, x, core, z] = value
        gram_rows[h, y] = value
    upper, lower = (lambda r: r.at[0:64]), (lambda r: r.at[64:PIECE_ROWS])

    def forward(ref):
        return courier.send(ref, ref, partner)

    hi_z = RingGather(
        courier, lambda p: upper(gram_cols.at[0, x, core, p]),
        lambda p: lower(gram_cols.at[0, x, core, p]), z, z_right, z_left,
    )
    lo_x = RingGather(
        courier, lambda p: upper(gram_cols.at[1, p, core, z]),
        lambda p: lower(gram_cols.at[1, p, core, z]), x, x_right, x_left,
    )
    rows_y = RingGather(
        courier, lambda p: gram_rows.at[0, p], lambda p: gram_rows.at[1, p], y, y_right, y_left,
    )
    hi_z.relay()
    lo_x.relay()
    hi_z.near()
    hi_z.far()
    hi_x = RingGather(
        courier, lambda p: gram_cols.at[0, p, core, 0:2],
        lambda p: gram_cols.at[0, p, core, 2:4], x, x_right, x_left,
    )
    across = [forward(gram_cols.at[0, x, core])]
    lo_x.near()
    lo_x.far()
    lo_z = RingGather(
        courier, lambda p: gram_cols.at[1, 0:2, core, p],
        lambda p: gram_cols.at[1, 2:4, core, p], z, z_right, z_left,
    )
    across.append(forward(gram_cols.at[1, :, core, z]))
    rows_y.relay()
    hi_x.relay()
    lo_z.relay()
    rows_y.near()
    rows_y.far()
    hi_x.near()
    for step in (1, 3):
        across.append(forward(gram_cols.at[0, mod(x + step, 4), core]))
    lo_z.near()
    for step in (1, 3):
        across.append(forward(gram_cols.at[1, :, core, mod(z + step, 4)]))
    hi_x.far()
    across.append(forward(gram_cols.at[0, mod(x + 2, 4), core]))
    lo_z.far()
    across.append(forward(gram_cols.at[1, :, core, mod(z + 2, 4)]))
    for copy in across:
        copy.wait_recv()

    square[...] = jnp.zeros_like(square)

    @pl.loop(0, 4)
    def _(m):
        high = gram_cols[0, m].reshape(PIECE_COLS, PIECE_COLS)
        low = gram_cols[1, m].reshape(PIECE_COLS, PIECE_COLS)
        left = jnp.concatenate([gram_rows[0, m], gram_rows[1, m]], axis=0)
        both = jnp.dot(left, high, preferred_element_type=f32)
        square[...] += (
            both[0:PIECE_ROWS] + both[PIECE_ROWS:]
            + jnp.dot(gram_rows[0, m], low, preferred_element_type=f32)
        )

    for h, value in enumerate(split(cubic_coef * gram_piece[...] + quintic_coef * square[...])):
        poly[h, y, z] = value
    hi_z = RingGather(
        courier, lambda p: upper(poly.at[0, y, p]), lambda p: lower(poly.at[0, y, p]),
        z, z_right, z_left,
    )
    lo_y = RingGather(
        courier, lambda p: upper(poly.at[1, p, z]), lambda p: lower(poly.at[1, p, z]),
        y, y_right, y_left,
    )
    hi_z.relay()
    lo_y.relay()
    hi_z.near()
    hi_z.far()
    hi_y = RingGather(
        courier, lambda p: poly.at[0, p, 0:2], lambda p: poly.at[0, p, 2:4], y, y_right, y_left,
    )
    lo_y.near()
    lo_y.far()
    lo_z = RingGather(
        courier, lambda p: poly.at[1, 0:2, p], lambda p: poly.at[1, 2:4, p], z, z_right, z_left,
    )
    hi_y.relay()
    lo_z.relay()
    hi_y.near()
    lo_z.near()
    hi_y.far()
    lo_z.far()

    block = y * 4 + z
    at_home = core == mod(y, 2)
    own = panel.at[x, pl.ds(pl.multiple_of(core * RB, RB), RB)]
    chunks = ((0, 512), (512, 640))
    offsets = [(dh, dz, dc) for dh in (1, 0) for dz in (2, 1, 3, 0) for dc in (1, 0)]

    def place(dh, dz, dc):
        y_to = core + 2 * mod(lax.div(y, jnp.int32(2)) + dh, 2)
        z_to, core_to = mod(z + dz, 4), mod(core + dc, 2)
        return y_to, z_to, core_to

    def window(source, low, size):
        return result.at[:, pl.ds(pl.multiple_of(source * WIDTH + low, 128), size)]

    def outward(chunk, index, offset):
        low, size = chunks[chunk]
        y_to, z_to, core_to = place(*offset)
        return pltpu.make_async_remote_copy(
            src_ref=outgoing.at[index, :, low:low + size],
            dst_ref=window(block, low, size),
            send_sem=out_send.at[chunk, index],
            recv_sem=out_recv.at[chunk, block],
            device_id=device(x, y_to, z_to, core_to),
            device_id_type=MESH,
        )

    row_ids = lax.broadcasted_iota(jnp.int32, (CAP, RB), 1)
    for index, offset in enumerate(offsets):
        y_to, z_to, core_to = place(*offset)
        g = (lax.div(y_to, jnp.int32(2)) * 4 + z_to) * 2 + core_to
        pick[index * CAP:(index + 1) * CAP] = (row_ids == slot_rows[g]).astype(f32)

    for chunk, (low, size) in enumerate(chunks):
        total = linear_coef * own[:, low:low + size].astype(f32)
        for m in range(4):
            for h in range(2):
                total = total + jnp.dot(
                    poly[h, m].reshape(RB, PIECE_COLS), panel[m, :, low:low + size],
                    preferred_element_type=f32,
                )
        high, rest = split(total)
        moved = jnp.dot(pick[...].astype(bf16), high, preferred_element_type=f32)
        moved = moved + jnp.dot(pick[...].astype(bf16), rest, preferred_element_type=f32)
        outgoing[:, :, low:low + size] = moved.reshape(16, CAP, size)
        for index, offset in enumerate(offsets):
            if any(offset):
                outward(chunk, index, offset).start()
            else:
                @pl.when(at_home)
                def _():
                    pltpu.make_async_copy(
                        outgoing.at[index, :, low:low + size], window(block, low, size),
                        out_recv.at[chunk, block],
                    ).start()

                @pl.when(jnp.logical_not(at_home))
                def _():
                    outward(chunk, index, offset).start()
    for chunk, (low, size) in enumerate(chunks):
        for source in range(16):
            pltpu.make_async_copy(
                window(source, low, size), window(source, low, size), out_recv.at[chunk, source]
            ).wait()
    courier.drain()
    for chunk in range(len(chunks)):
        for index, offset in enumerate(offsets):
            if any(offset):
                outward(chunk, index, offset).wait_send()
            else:
                @pl.when(jnp.logical_not(at_home))
                def _():
                    outward(chunk, index, offset).wait_send()


VMEM_LIMIT = 64000 * 1024
in_vmem = pl.BlockSpec(memory_space=pltpu.VMEM)
anywhere = pl.BlockSpec(memory_space=pl.ANY)


def body(shards, counts):
    x, _, _, core = position()
    row_block = x * 2 + core
    my_counts = lax.dynamic_slice_in_dim(counts, row_block, 1, 0)
    my_starts = jnp.cumsum(my_counts, axis=1) - my_counts
    slots = jnp.arange(CAP, dtype=jnp.int32)[None, :]
    target_rows = jnp.where(
        slots < my_counts[0][:, None], my_starts[0][:, None] + slots, -1
    ).reshape(1, 16 * CAP)

    panel, gram_piece = pl.pallas_call(
        gram_kernel,
        name="gram_kernel",
        out_shape=(
            jax.ShapeDtypeStruct((4, 2 * RB, WIDTH), bf16),
            jax.ShapeDtypeStruct((PIECE_ROWS, PIECE_COLS), f32),
        ),
        in_specs=[anywhere, in_vmem],
        out_specs=(in_vmem, in_vmem),
        scratch_shapes=[
            pltpu.VMEM((16, CAP, WIDTH), bf16),
            pltpu.VMEM((16 * CAP, WIDTH), f32),
            pltpu.VMEM((4, 4, 2, CAP, PIECE_COLS), f32),
            pltpu.VMEM((2, 2, 2, CAP, PIECE_COLS), f32),
            pltpu.VMEM((2, 2, 4, CAP, PIECE_COLS), f32),
            pltpu.VMEM((2, 32, PIECE_COLS), f32),
            pltpu.VMEM((2, CAP - 32, PIECE_COLS), f32),
            pltpu.VMEM((2, 2, CAP, PIECE_COLS), f32),
            pltpu.SemaphoreType.DMA((40,)),
            pltpu.SemaphoreType.DMA((40,)),
            pltpu.SemaphoreType.DMA((16,)),
            pltpu.SemaphoreType.DMA((16,)),
        ],
        compiler_params=pltpu.CompilerParams(
            collective_id=0, has_side_effects=True, vmem_limit_bytes=VMEM_LIMIT
        ),
    )(shards[0, 0], target_rows)

    result = pl.pallas_call(
        update_kernel,
        name="update_kernel",
        out_shape=jax.ShapeDtypeStruct((CAP, N), f32),
        in_specs=[in_vmem, in_vmem, in_vmem],
        out_specs=anywhere,
        scratch_shapes=[
            pltpu.VMEM((2, 4, 2, 4, PIECE_ROWS, PIECE_COLS), bf16),
            pltpu.VMEM((2, 4, PIECE_ROWS, PIECE_COLS), bf16),
            pltpu.VMEM((PIECE_ROWS, PIECE_COLS), f32),
            pltpu.VMEM((2, 4, 4, PIECE_ROWS, PIECE_COLS), bf16),
            pltpu.VMEM((16 * CAP, RB), f32),
            pltpu.VMEM((16, CAP, WIDTH), f32),
            pltpu.SemaphoreType.DMA((64,)),
            pltpu.SemaphoreType.DMA((64,)),
            pltpu.SemaphoreType.DMA((2, 16)),
            pltpu.SemaphoreType.DMA((2, 16)),
        ],
        compiler_params=pltpu.CompilerParams(
            collective_id=1, has_side_effects=True, vmem_limit_bytes=VMEM_LIMIT
        ),
    )(target_rows.reshape(16, CAP, 1), gram_piece, panel)
    return result.reshape(1, 1, CAP, N)


def solution(mesh):
    placed = (P("gr", "gc", None, None), P())
    return jax.shard_map(
        body, mesh=mesh, in_specs=placed, out_specs=P("gr", "gc", None, None), check_vma=False
    )
```

```python
import jax
import jax.numpy as jnp
from jax import lax
from jax.experimental import pallas as pl
from jax.experimental.pallas import tpu as pltpu
from jax.sharding import PartitionSpec as P

M = 3584
N = 18432
CAP = 56
RB = 448
WIDTH = 1152
PIECE_ROWS = 112
PIECE_COLS = 896

linear_coef = 3.4445
cubic_coef = -4.775
quintic_coef = 2.0315

MESH = pl.DeviceIdType.MESH
f32 = jnp.float32
bf16 = jnp.bfloat16


def mod(value, size):
    return lax.rem(value, jnp.int32(size))


def position():
    gr = lax.axis_index("gr")
    gc = lax.axis_index("gc")
    half = lax.div(gr, jnp.int32(2))
    x = lax.div(gc, jnp.int32(2))
    y = lax.div(half, jnp.int32(4)) * 2 + mod(gc, 2)
    return x, y, mod(half, 4), mod(gr, 2)


def device(x, y, z, core):
    return {
        "gr": (lax.div(y, jnp.int32(2)) * 4 + z) * 2 + core,
        "gc": x * 2 + mod(y, 2),
    }


def greet(x, y, z, core):
    barrier = pltpu.get_barrier_semaphore()
    count = 0
    for dy in range(4):
        for dz in range(4):
            for dc in range(2):
                if dy or dz or dc:
                    target = device(x, mod(y + dy, 4), mod(z + dz, 4), mod(core + dc, 2))
                    pl.semaphore_signal(barrier, inc=1, device_id=target, device_id_type=MESH)
                    count += 1
    for dx in (1, 3):
        target = device(mod(x + dx, 4), y, z, core)
        pl.semaphore_signal(barrier, inc=1, device_id=target, device_id_type=MESH)
        count += 1
    pl.semaphore_wait(barrier, count)


class Courier:
    def __init__(self, send_sem, recv_sem):
        self.send_sem, self.recv_sem = send_sem, recv_sem
        self.copies = []

    def send(self, src, dst, target):
        index = len(self.copies)
        copy = pltpu.make_async_remote_copy(
            src_ref=src,
            dst_ref=dst,
            send_sem=self.send_sem.at[index],
            recv_sem=self.recv_sem.at[index],
            device_id=target,
            device_id_type=MESH,
        )
        self.copies.append(copy)
        copy.start()
        return copy

    def drain(self):
        for copy in self.copies:
            copy.wait_send()


class RingGather:
    def __init__(self, courier, part_a, part_b, pos, right, left):
        self.courier, self.part_a, self.part_b = courier, part_a, part_b
        self.pos, self.right, self.left = pos, right, left
        a, b = part_a(pos), part_b(pos)
        self.a_right = courier.send(a, a, right)
        self.b_left = courier.send(b, b, left)
        self.b_right = courier.send(b, b, right)
        self.a_left = courier.send(a, a, left)

    def relay(self):
        self.a_right.wait_recv()
        a = self.part_a(mod(self.pos + 3, 4))
        self.a_far = self.courier.send(a, a, self.right)
        self.b_left.wait_recv()
        b = self.part_b(mod(self.pos + 1, 4))
        self.b_far = self.courier.send(b, b, self.left)

    def near(self):
        self.b_right.wait_recv()
        self.a_left.wait_recv()

    def far(self):
        self.a_far.wait_recv()
        self.b_far.wait_recv()


class RingReduce:
    def __init__(self, courier, part_a, part_b, bufs, cut, pos, right, left):
        self.courier, self.part_a, self.part_b = courier, part_a, part_b
        self.pos, self.right, self.left = pos, right, left
        self.tmp_a, self.tmp_b, self.from_left, self.from_right = bufs
        self.in_a, self.in_b = cut
        far = mod(pos + 2, 4)
        self.a1 = courier.send(part_a(far), self.tmp_a, right)
        self.b1 = courier.send(part_b(far), self.tmp_b, left)
        self.a2 = courier.send(part_b(mod(pos + 1, 4)), self.in_b(self.from_left), right)
        self.b2 = courier.send(part_a(mod(pos + 3, 4)), self.in_a(self.from_right), left)

    def relay(self):
        self.a1.wait_recv()
        a = self.part_a(mod(self.pos + 1, 4))
        a[...] = a[...] + self.tmp_a[...]
        self.a3 = self.courier.send(a, self.in_a(self.from_left), self.right)
        self.b1.wait_recv()
        b = self.part_b(mod(self.pos + 3, 4))
        b[...] = b[...] + self.tmp_b[...]
        self.b3 = self.courier.send(b, self.in_b(self.from_right), self.left)

    def finish(self):
        for copy in (self.a2, self.b2, self.a3, self.b3):
            copy.wait_recv()


def gram_kernel(
    shard, target_rows, panel, gram_piece, received, wide, part,
    big_tmp, big_recv, small_tmp_a, small_tmp_b, small_recv,
    relay, send_sem, recv_sem, in_send, in_recv, relay_send, relay_recv,
):
    x, y, z, core = position()
    greet(x, y, z, core)
    y_lo = mod(y, 2)
    me = lax.axis_index("gr")
    at_home = core == y_lo

    def columns(dy, dz):
        block = mod(y + dy, 4) * 4 + mod(z + dz, 4)
        return shard.at[:, pl.ds(pl.multiple_of(block * WIDTH, 128), WIDTH)]

    def outward(index, dy, dz):
        return pltpu.make_async_remote_copy(
            src_ref=columns(dy, dz),
            dst_ref=received.at[me],
            send_sem=in_send.at[index],
            recv_sem=in_recv.at[me],
            device_id=device(x, mod(y + dy, 4), mod(z + dz, 4), y_lo),
            device_id_type=MESH,
        )

    offsets = [(dy, dz) for dy in range(4) for dz in range(4)]
    offsets = sorted(offsets, key=lambda o: -(min(o[0], 4 - o[0]) + min(o[1], 4 - o[1])))
    detours = {(2, 2): (3, 3), (3, 2): (0, 3), (2, 3): (3, 0)}
    offsets = list(detours) + [o for o in offsets if o not in detours]

    def first_leg(index):
        vy, vz = detours[offsets[index]]
        return pltpu.make_async_remote_copy(
            src_ref=columns(*offsets[index]),
            dst_ref=relay.at[index],
            send_sem=in_send.at[index],
            recv_sem=relay_recv.at[index],
            device_id=device(x, mod(y + vy, 4), mod(z + vz, 4), core),
            device_id_type=MESH,
        )

    def second_leg(index):
        dy, dz = offsets[index]
        vy, vz = detours[offsets[index]]
        y_from, z_from = mod(y + 4 - vy, 4), mod(z + 4 - vz, 4)
        source = device(x, y_from, z_from, core)["gr"]
        return pltpu.make_async_remote_copy(
            src_ref=relay.at[index],
            dst_ref=received.at[source],
            send_sem=relay_send.at[index],
            recv_sem=in_recv.at[source],
            device_id=device(x, mod(y_from + dy, 4), mod(z_from + dz, 4), mod(y_from, 2)),
            device_id_type=MESH,
        )

    for index, (dy, dz) in enumerate(offsets):
        if (dy, dz) in detours:
            first_leg(index).start()
        elif dy or dz:
            outward(index, dy, dz).start()
        else:
            @pl.when(at_home)
            def _():
                pltpu.make_async_copy(columns(0, 0), received.at[me], in_recv.at[me]).start()

            @pl.when(jnp.logical_not(at_home))
            def _():
                outward(index, 0, 0).start()
    for index in range(len(detours)):
        first_leg(index).wait_recv()
        second_leg(index).start()
    for g in range(16):
        pltpu.make_async_copy(received.at[g], received.at[g], in_recv.at[g]).wait()
        wide[g * CAP:(g + 1) * CAP] = received[g].astype(f32)

    rows = lax.broadcasted_iota(jnp.int32, (RB, 16 * CAP), 0)
    pick = (rows == target_rows[...]).astype(f32).astype(bf16)
    own = panel.at[x, pl.ds(pl.multiple_of(core * RB, RB), RB)]
    for low, size in ((0, 512), (512, 640)):
        own[:, low:low + size] = jnp.dot(
            pick, wide[:, low:low + size].astype(bf16), preferred_element_type=f32
        ).astype(bf16)

    courier = Courier(send_sem, recv_sem)
    partner = device(x, y, z, 1 - core)

    def slot(low):
        def part_of(pos):
            return panel.at[pos, pl.ds(pl.multiple_of(core * RB + low, 32), RB // 2)]
        return part_of

    def whole(pos):
        return panel.at[pos, pl.ds(pl.multiple_of(core * RB, 32), RB)]

    ring = RingGather(
        courier, slot(0), slot(RB // 2), x,
        device(mod(x + 1, 4), y, z, core), device(mod(x + 3, 4), y, z, core),
    )
    across = [courier.send(whole(x), whole(x), partner)]

    def multiply(pos):
        product = lax.dot_general(
            own[...], panel[pos], (((1,), (1,)), ((), ())), preferred_element_type=f32
        )
        part[pos] = (product * (1.0 / N)).reshape(4, 2, CAP, PIECE_COLS)

    ring.relay()
    ring.near()
    for step in (1, 3):
        pos = mod(x + step, 4)
        across.append(courier.send(whole(pos), whole(pos), partner))
    across[0].wait_recv()
    multiply(x)
    across[1].wait_recv()
    multiply(mod(x + 1, 4))
    across[2].wait_recv()
    multiply(mod(x + 3, 4))
    ring.far()
    pos = mod(x + 2, 4)
    across.append(courier.send(whole(pos), whole(pos), partner))
    across[3].wait_recv()
    multiply(pos)

    z_right, z_left = device(x, y, mod(z + 1, 4), core), device(x, y, mod(z + 3, 4), core)
    y_right, y_left = device(x, mod(y + 1, 4), z, core), device(x, mod(y + 3, 4), z, core)
    first, second = (lambda r: r.at[0:2]), (lambda r: r.at[2:4])
    upper, lower = (lambda r: r.at[0:32]), (lambda r: r.at[32:CAP])

    def bufs(tmp_a, tmp_b, recv, half):
        return tmp_a.at[half], tmp_b.at[half], recv.at[half, 0], recv.at[half, 1]

    big = lambda half: bufs(big_tmp.at[0], big_tmp.at[1], big_recv, half)
    small = lambda half: bufs(small_tmp_a, small_tmp_b, small_recv, half)
    one = RingReduce(
        courier, lambda p: part.at[0:2, p, 0], lambda p: part.at[2:4, p, 0],
        big(0), (first, second), z, z_right, z_left,
    )
    two = RingReduce(
        courier, lambda p: part.at[p, 0:2, 1], lambda p: part.at[p, 2:4, 1],
        big(1), (first, second), y, y_right, y_left,
    )
    one.relay()
    two.relay()
    one.finish()
    part[:, z, 0] = part[:, z, 0] + big_recv[0, 0] + big_recv[0, 1]
    three = RingReduce(
        courier, lambda p: upper(part.at[p, z, 0]), lambda p: lower(part.at[p, z, 0]),
        small(0), (upper, lower), y, y_right, y_left,
    )
    two.finish()
    part[y, :, 1] = part[y, :, 1] + big_recv[1, 0] + big_recv[1, 1]
    four = RingReduce(
        courier, lambda p: upper(part.at[y, p, 1]), lambda p: lower(part.at[y, p, 1]),
        small(1), (upper, lower), z, z_right, z_left,
    )
    three.relay()
    four.relay()
    three.finish()
    gram_piece[0:CAP] = part[y, z, 0] + small_recv[0, 0] + small_recv[0, 1]
    four.finish()
    gram_piece[CAP:2 * CAP] = part[y, z, 1] + small_recv[1, 0] + small_recv[1, 1]
    courier.drain()
    for index, (dy, dz) in enumerate(offsets):
        if (dy, dz) in detours:
            first_leg(index).wait_send()
            second_leg(index).wait_send()
        elif dy or dz:
            outward(index, dy, dz).wait_send()
        else:
            @pl.when(jnp.logical_not(at_home))
            def _():
                outward(index, 0, 0).wait_send()


def split(value):
    high = value.astype(bf16)
    return high, (value - high.astype(f32)).astype(bf16)


def update_kernel(
    slot_rows, gram_piece, panel, result, gram_cols, gram_rows, square, poly,
    pick, outgoing, relay, send_sem, recv_sem, out_send, out_recv,
    relay_recv, relay_send,
):
    x, y, z, core = position()
    greet(x, y, z, core)
    courier = Courier(send_sem, recv_sem)
    partner = device(x, y, z, 1 - core)
    z_right, z_left = device(x, y, mod(z + 1, 4), core), device(x, y, mod(z + 3, 4), core)
    y_right, y_left = device(x, mod(y + 1, 4), z, core), device(x, mod(y + 3, 4), z, core)
    x_right, x_left = device(mod(x + 1, 4), y, z, core), device(mod(x + 3, 4), y, z, core)

    for h, value in enumerate(split(gram_piece[...])):
        gram_cols[h, x, core, z] = value
        gram_rows[h, y] = value
    upper, lower = (lambda r: r.at[0:64]), (lambda r: r.at[64:PIECE_ROWS])

    def forward(ref):
        return courier.send(ref, ref, partner)

    hi_z = RingGather(
        courier, lambda p: upper(gram_cols.at[0, x, core, p]),
        lambda p: lower(gram_cols.at[0, x, core, p]), z, z_right, z_left,
    )
    lo_x = RingGather(
        courier, lambda p: upper(gram_cols.at[1, p, core, z]),
        lambda p: lower(gram_cols.at[1, p, core, z]), x, x_right, x_left,
    )
    rows_y = RingGather(
        courier, lambda p: gram_rows.at[0, p], lambda p: gram_rows.at[1, p], y, y_right, y_left,
    )
    hi_z.relay()
    lo_x.relay()
    hi_z.near()
    hi_z.far()
    hi_x = RingGather(
        courier, lambda p: gram_cols.at[0, p, core, 0:2],
        lambda p: gram_cols.at[0, p, core, 2:4], x, x_right, x_left,
    )
    across = [forward(gram_cols.at[0, x, core])]
    lo_x.near()
    lo_x.far()
    lo_z = RingGather(
        courier, lambda p: gram_cols.at[1, 0:2, core, p],
        lambda p: gram_cols.at[1, 2:4, core, p], z, z_right, z_left,
    )
    across.append(forward(gram_cols.at[1, :, core, z]))
    rows_y.relay()
    hi_x.relay()
    lo_z.relay()
    rows_y.near()
    rows_y.far()
    hi_x.near()
    for step in (1, 3):
        across.append(forward(gram_cols.at[0, mod(x + step, 4), core]))
    lo_z.near()
    for step in (1, 3):
        across.append(forward(gram_cols.at[1, :, core, mod(z + step, 4)]))
    hi_x.far()
    across.append(forward(gram_cols.at[0, mod(x + 2, 4), core]))
    lo_z.far()
    across.append(forward(gram_cols.at[1, :, core, mod(z + 2, 4)]))
    for copy in across:
        copy.wait_recv()

    square[...] = jnp.zeros_like(square)

    @pl.loop(0, 4)
    def _(m):
        high = gram_cols[0, m].reshape(PIECE_COLS, PIECE_COLS)
        low = gram_cols[1, m].reshape(PIECE_COLS, PIECE_COLS)
        left = jnp.concatenate([gram_rows[0, m], gram_rows[1, m]], axis=0)
        both = jnp.dot(left, high, preferred_element_type=f32)
        square[...] += (
            both[0:PIECE_ROWS] + both[PIECE_ROWS:]
            + jnp.dot(gram_rows[0, m], low, preferred_element_type=f32)
        )

    for h, value in enumerate(split(cubic_coef * gram_piece[...] + quintic_coef * square[...])):
        poly[h, y, z] = value
    hi_z = RingGather(
        courier, lambda p: upper(poly.at[0, y, p]), lambda p: lower(poly.at[0, y, p]),
        z, z_right, z_left,
    )
    lo_y = RingGather(
        courier, lambda p: upper(poly.at[1, p, z]), lambda p: lower(poly.at[1, p, z]),
        y, y_right, y_left,
    )
    hi_z.relay()
    lo_y.relay()
    hi_z.near()
    hi_z.far()
    hi_y = RingGather(
        courier, lambda p: poly.at[0, p, 0:2], lambda p: poly.at[0, p, 2:4], y, y_right, y_left,
    )
    lo_y.near()
    lo_y.far()
    lo_z = RingGather(
        courier, lambda p: poly.at[1, 0:2, p], lambda p: poly.at[1, 2:4, p], z, z_right, z_left,
    )
    hi_y.relay()
    lo_z.relay()
    hi_y.near()
    lo_z.near()
    hi_y.far()
    lo_z.far()

    block = y * 4 + z
    at_home = core == mod(y, 2)
    own = panel.at[x, pl.ds(pl.multiple_of(core * RB, RB), RB)]
    chunks = ((0, 256), (256, 384), (640, 512))
    offsets = [(dh, dz, dc) for dh in (1, 0) for dz in (2, 1, 3, 0) for dc in (1, 0)]
    detours = [(1, 2, 1), (0, 2, 1), (1, 1, 1), (1, 3, 1), (1, 0, 1)]
    offsets = detours + [o for o in offsets if o not in detours]

    def place(dh, dz, dc, y_from=y, z_from=z):
        y_to = core + 2 * mod(lax.div(y_from, jnp.int32(2)) + dh, 2)
        z_to, core_to = mod(z_from + dz, 4), mod(core + dc, 2)
        return y_to, z_to, core_to

    def window(source, low, size):
        return result.at[:, pl.ds(pl.multiple_of(source * WIDTH + low, 128), size)]

    def outward(chunk, index, offset):
        low, size = chunks[chunk]
        y_to, z_to, core_to = place(*offset)
        return pltpu.make_async_remote_copy(
            src_ref=outgoing.at[index, :, low:low + size],
            dst_ref=window(block, low, size),
            send_sem=out_send.at[chunk, index],
            recv_sem=out_recv.at[chunk, block],
            device_id=device(x, y_to, z_to, core_to),
            device_id_type=MESH,
        )

    def relay_at(index):
        side = 1 + 2 * core
        if index == 0:
            return (
                mod(y + jnp.where(at_home, 3, side), 4), mod(z + 3, 4),
                mod(y + jnp.where(at_home, 4 - side, 1), 4), mod(z + 1, 4),
            )
        if index == 1:
            return y, mod(z + 3, 4), y, mod(z + 1, 4)
        return mod(y + 3, 4), z, mod(y + 1, 4), z

    def first_leg(chunk, index):
        low, size = chunks[chunk]
        y_to, z_to, _, _ = relay_at(index)
        return pltpu.make_async_remote_copy(
            src_ref=outgoing.at[index, :, low:low + size],
            dst_ref=relay.at[index, :, low:low + size],
            send_sem=out_send.at[chunk, index],
            recv_sem=relay_recv.at[chunk, index],
            device_id=device(x, y_to, z_to, core),
            device_id_type=MESH,
        )

    def second_leg(chunk, index):
        low, size = chunks[chunk]
        _, _, y_from, z_from = relay_at(index)
        y_to, z_to, core_to = place(*offsets[index], y_from, z_from)
        source = y_from * 4 + z_from
        return pltpu.make_async_remote_copy(
            src_ref=relay.at[index, :, low:low + size],
            dst_ref=window(source, low, size),
            send_sem=relay_send.at[chunk, index],
            recv_sem=out_recv.at[chunk, source],
            device_id=device(x, y_to, z_to, core_to),
            device_id_type=MESH,
        )

    def pass_on(chunk):
        for index in range(len(detours)):
            if index < 2:
                first_leg(chunk, index).wait_recv()
                second_leg(chunk, index).start()
            else:
                @pl.when(jnp.logical_not(at_home))
                def _():
                    first_leg(chunk, index).wait_recv()
                    second_leg(chunk, index).start()

    row_ids = lax.broadcasted_iota(jnp.int32, (CAP, RB), 1)
    for index, offset in enumerate(offsets):
        y_to, z_to, core_to = place(*offset)
        g = (lax.div(y_to, jnp.int32(2)) * 4 + z_to) * 2 + core_to
        pick[index * CAP:(index + 1) * CAP] = (row_ids == slot_rows[g]).astype(f32)

    for chunk, (low, size) in enumerate(chunks):
        total = linear_coef * own[:, low:low + size].astype(f32)
        for m in range(4):
            for h in range(2):
                total = total + jnp.dot(
                    poly[h, m].reshape(RB, PIECE_COLS), panel[m, :, low:low + size],
                    preferred_element_type=f32,
                )
        high, rest = split(total)
        moved = jnp.dot(pick[...].astype(bf16), high, preferred_element_type=f32)
        moved = moved + jnp.dot(pick[...].astype(bf16), rest, preferred_element_type=f32)
        outgoing[:, :, low:low + size] = moved.reshape(16, CAP, size)
        for index, offset in enumerate(offsets):
            if index < 2:
                first_leg(chunk, index).start()
            elif index < len(detours):
                @pl.when(at_home)
                def _():
                    first_leg(chunk, index).start()

                @pl.when(jnp.logical_not(at_home))
                def _():
                    outward(chunk, index, offset).start()
            elif any(offset):
                outward(chunk, index, offset).start()
            else:
                @pl.when(at_home)
                def _():
                    pltpu.make_async_copy(
                        outgoing.at[index, :, low:low + size], window(block, low, size),
                        out_recv.at[chunk, block],
                    ).start()

                @pl.when(jnp.logical_not(at_home))
                def _():
                    outward(chunk, index, offset).start()
        if chunk:
            pass_on(chunk - 1)
    pass_on(len(chunks) - 1)
    for chunk, (low, size) in enumerate(chunks):
        for source in range(16):
            pltpu.make_async_copy(
                window(source, low, size), window(source, low, size), out_recv.at[chunk, source]
            ).wait()
    courier.drain()
    for chunk in range(len(chunks)):
        for index, offset in enumerate(offsets):
            if index < 2:
                first_leg(chunk, index).wait_send()
                second_leg(chunk, index).wait_send()
            elif index < len(detours):
                @pl.when(at_home)
                def _():
                    first_leg(chunk, index).wait_send()

                @pl.when(jnp.logical_not(at_home))
                def _():
                    outward(chunk, index, offset).wait_send()
                    second_leg(chunk, index).wait_send()
            elif any(offset):
                outward(chunk, index, offset).wait_send()
            else:
                @pl.when(jnp.logical_not(at_home))
                def _():
                    outward(chunk, index, offset).wait_send()


VMEM_LIMIT = 64000 * 1024
in_vmem = pl.BlockSpec(memory_space=pltpu.VMEM)
anywhere = pl.BlockSpec(memory_space=pl.ANY)


def body(shards, counts):
    x, _, _, core = position()
    row_block = x * 2 + core
    my_counts = lax.dynamic_slice_in_dim(counts, row_block, 1, 0)
    my_starts = jnp.cumsum(my_counts, axis=1) - my_counts
    slots = jnp.arange(CAP, dtype=jnp.int32)[None, :]
    target_rows = jnp.where(
        slots < my_counts[0][:, None], my_starts[0][:, None] + slots, -1
    ).reshape(1, 16 * CAP)

    panel, gram_piece = pl.pallas_call(
        gram_kernel,
        name="gram_kernel",
        out_shape=(
            jax.ShapeDtypeStruct((4, 2 * RB, WIDTH), bf16),
            jax.ShapeDtypeStruct((PIECE_ROWS, PIECE_COLS), f32),
        ),
        in_specs=[anywhere, in_vmem],
        out_specs=(in_vmem, in_vmem),
        scratch_shapes=[
            pltpu.VMEM((16, CAP, WIDTH), bf16),
            pltpu.VMEM((16 * CAP, WIDTH), f32),
            pltpu.VMEM((4, 4, 2, CAP, PIECE_COLS), f32),
            pltpu.VMEM((2, 2, 2, CAP, PIECE_COLS), f32),
            pltpu.VMEM((2, 2, 4, CAP, PIECE_COLS), f32),
            pltpu.VMEM((2, 32, PIECE_COLS), f32),
            pltpu.VMEM((2, CAP - 32, PIECE_COLS), f32),
            pltpu.VMEM((2, 2, CAP, PIECE_COLS), f32),
            pltpu.VMEM((3, CAP, WIDTH), bf16),
            pltpu.SemaphoreType.DMA((40,)),
            pltpu.SemaphoreType.DMA((40,)),
            pltpu.SemaphoreType.DMA((16,)),
            pltpu.SemaphoreType.DMA((16,)),
            pltpu.SemaphoreType.DMA((3,)),
            pltpu.SemaphoreType.DMA((3,)),
        ],
        compiler_params=pltpu.CompilerParams(
            collective_id=0, has_side_effects=True, vmem_limit_bytes=VMEM_LIMIT
        ),
    )(shards[0, 0], target_rows)

    result = pl.pallas_call(
        update_kernel,
        name="update_kernel",
        out_shape=jax.ShapeDtypeStruct((CAP, N), f32),
        in_specs=[in_vmem, in_vmem, in_vmem],
        out_specs=anywhere,
        scratch_shapes=[
            pltpu.VMEM((2, 4, 2, 4, PIECE_ROWS, PIECE_COLS), bf16),
            pltpu.VMEM((2, 4, PIECE_ROWS, PIECE_COLS), bf16),
            pltpu.VMEM((PIECE_ROWS, PIECE_COLS), f32),
            pltpu.VMEM((2, 4, 4, PIECE_ROWS, PIECE_COLS), bf16),
            pltpu.VMEM((16 * CAP, RB), f32),
            pltpu.VMEM((16, CAP, WIDTH), f32),
            pltpu.VMEM((5, CAP, WIDTH), f32),
            pltpu.SemaphoreType.DMA((64,)),
            pltpu.SemaphoreType.DMA((64,)),
            pltpu.SemaphoreType.DMA((3, 16)),
            pltpu.SemaphoreType.DMA((3, 16)),
            pltpu.SemaphoreType.DMA((3, 5)),
            pltpu.SemaphoreType.DMA((3, 5)),
        ],
        compiler_params=pltpu.CompilerParams(
            collective_id=1, has_side_effects=True, vmem_limit_bytes=VMEM_LIMIT
        ),
    )(target_rows.reshape(16, CAP, 1), gram_piece, panel)
    return result.reshape(1, 1, CAP, N)


def solution(mesh):
    placed = (P("gr", "gc", None, None), P())
    return jax.shard_map(
        body, mesh=mesh, in_specs=placed, out_specs=P("gr", "gc", None, None), check_vma=False
    )
```

```python
import jax
import jax.numpy as jnp
from jax import lax
from jax.experimental import pallas as pl
from jax.experimental.pallas import tpu as pltpu
from jax.sharding import PartitionSpec as P

M = 3584
N = 18432
CAP = 56
RB = 448
WIDTH = 1152
PIECE_ROWS = 112
PIECE_COLS = 896

linear_coef = 3.4445
cubic_coef = -4.775
quintic_coef = 2.0315

MESH = pl.DeviceIdType.MESH
f32 = jnp.float32
bf16 = jnp.bfloat16


def mod(value, size):
    return lax.rem(value, jnp.int32(size))


def position():
    gr = lax.axis_index("gr")
    gc = lax.axis_index("gc")
    half = lax.div(gr, jnp.int32(2))
    x = lax.div(gc, jnp.int32(2))
    y = lax.div(half, jnp.int32(4)) * 2 + mod(gc, 2)
    return x, y, mod(half, 4), mod(gr, 2)


def device(x, y, z, core):
    return {
        "gr": (lax.div(y, jnp.int32(2)) * 4 + z) * 2 + core,
        "gc": x * 2 + mod(y, 2),
    }


def greet(x, y, z, core):
    barrier = pltpu.get_barrier_semaphore()
    count = 0
    for dy in range(4):
        for dz in range(4):
            for dc in range(2):
                if dy or dz or dc:
                    target = device(x, mod(y + dy, 4), mod(z + dz, 4), mod(core + dc, 2))
                    pl.semaphore_signal(barrier, inc=1, device_id=target, device_id_type=MESH)
                    count += 1
    for dx in (1, 3):
        target = device(mod(x + dx, 4), y, z, core)
        pl.semaphore_signal(barrier, inc=1, device_id=target, device_id_type=MESH)
        count += 1
    pl.semaphore_wait(barrier, count)


class Courier:
    def __init__(self, send_sem, recv_sem):
        self.send_sem, self.recv_sem = send_sem, recv_sem
        self.copies = []

    def send(self, src, dst, target):
        index = len(self.copies)
        copy = pltpu.make_async_remote_copy(
            src_ref=src,
            dst_ref=dst,
            send_sem=self.send_sem.at[index],
            recv_sem=self.recv_sem.at[index],
            device_id=target,
            device_id_type=MESH,
        )
        self.copies.append(copy)
        copy.start()
        return copy

    def drain(self):
        for copy in self.copies:
            copy.wait_send()


class RingGather:
    def __init__(self, courier, part_a, part_b, pos, right, left):
        self.courier, self.part_a, self.part_b = courier, part_a, part_b
        self.pos, self.right, self.left = pos, right, left
        a, b = part_a(pos), part_b(pos)
        self.a_right = courier.send(a, a, right)
        self.b_left = courier.send(b, b, left)
        self.b_right = courier.send(b, b, right)
        self.a_left = courier.send(a, a, left)

    def relay(self):
        self.a_right.wait_recv()
        a = self.part_a(mod(self.pos + 3, 4))
        self.a_far = self.courier.send(a, a, self.right)
        self.b_left.wait_recv()
        b = self.part_b(mod(self.pos + 1, 4))
        self.b_far = self.courier.send(b, b, self.left)

    def near(self):
        self.b_right.wait_recv()
        self.a_left.wait_recv()

    def far(self):
        self.a_far.wait_recv()
        self.b_far.wait_recv()


class RingReduce:
    def __init__(self, courier, part_a, part_b, bufs, cut, pos, right, left):
        self.courier, self.part_a, self.part_b = courier, part_a, part_b
        self.pos, self.right, self.left = pos, right, left
        self.tmp_a, self.tmp_b, self.from_left, self.from_right = bufs
        self.in_a, self.in_b = cut
        far = mod(pos + 2, 4)
        self.a1 = courier.send(part_a(far), self.tmp_a, right)
        self.b1 = courier.send(part_b(far), self.tmp_b, left)
        self.a2 = courier.send(part_b(mod(pos + 1, 4)), self.in_b(self.from_left), right)
        self.b2 = courier.send(part_a(mod(pos + 3, 4)), self.in_a(self.from_right), left)

    def relay(self):
        self.a1.wait_recv()
        a = self.part_a(mod(self.pos + 1, 4))
        a[...] = a[...] + self.tmp_a[...]
        self.a3 = self.courier.send(a, self.in_a(self.from_left), self.right)
        self.b1.wait_recv()
        b = self.part_b(mod(self.pos + 3, 4))
        b[...] = b[...] + self.tmp_b[...]
        self.b3 = self.courier.send(b, self.in_b(self.from_right), self.left)

    def finish(self):
        for copy in (self.a2, self.b2, self.a3, self.b3):
            copy.wait_recv()


def gram_kernel(
    shard, target_rows, panel, gram_piece, received, wide, part,
    big_tmp, big_recv, small_tmp_a, small_tmp_b, small_recv,
    send_sem, recv_sem, in_send, in_recv,
):
    x, y, z, core = position()
    greet(x, y, z, core)
    y_lo = mod(y, 2)
    me = lax.axis_index("gr")
    at_home = core == y_lo

    chunks = ((0, 512), (512, 640))

    def columns(chunk, dy, dz):
        low, size = chunks[chunk]
        block = mod(y + dy, 4) * 4 + mod(z + dz, 4)
        return shard.at[:, pl.ds(pl.multiple_of(block * WIDTH + low, 128), size)]

    def landing(chunk, source):
        low, size = chunks[chunk]
        return received.at[source, :, low:low + size]

    def outward(chunk, index, dy, dz):
        return pltpu.make_async_remote_copy(
            src_ref=columns(chunk, dy, dz),
            dst_ref=landing(chunk, me),
            send_sem=in_send.at[chunk, index],
            recv_sem=in_recv.at[chunk, me],
            device_id=device(x, mod(y + dy, 4), mod(z + dz, 4), y_lo),
            device_id_type=MESH,
        )

    offsets = [(dy, dz) for dy in range(4) for dz in range(4)]
    offsets = sorted(offsets, key=lambda o: -(min(o[0], 4 - o[0]) + min(o[1], 4 - o[1])))
    for chunk in range(2):
        for index, (dy, dz) in enumerate(offsets):
            if dy or dz:
                outward(chunk, index, dy, dz).start()
            else:
                @pl.when(at_home)
                def _():
                    pltpu.make_async_copy(
                        columns(chunk, 0, 0), landing(chunk, me), in_recv.at[chunk, me]
                    ).start()

                @pl.when(jnp.logical_not(at_home))
                def _():
                    outward(chunk, index, 0, 0).start()

    courier = Courier(send_sem, recv_sem)
    partner = device(x, y, z, 1 - core)
    x_right, x_left = device(mod(x + 1, 4), y, z, core), device(mod(x + 3, 4), y, z, core)
    rows = lax.broadcasted_iota(jnp.int32, (RB, 16 * CAP), 0)
    own = panel.at[x, pl.ds(pl.multiple_of(core * RB, RB), RB)]
    across = [[], []]

    def assemble(chunk):
        low, size = chunks[chunk]
        for g in range(16):
            pltpu.make_async_copy(
                landing(chunk, g), landing(chunk, g), in_recv.at[chunk, g]
            ).wait()
            wide[g * CAP:(g + 1) * CAP, low:low + size] = (
                received[g, :, low:low + size].astype(f32)
            )
        pick = (rows == target_rows[...]).astype(f32).astype(bf16)
        own[:, low:low + size] = jnp.dot(
            pick, wide[:, low:low + size].astype(bf16), preferred_element_type=f32
        ).astype(bf16)

    def rows_of(chunk, first, count):
        low, size = chunks[chunk]

        def part_of(pos):
            start = pl.multiple_of(core * RB + first, 32)
            return panel.at[pos, pl.ds(start, count), low:low + size]
        return part_of

    def ring(chunk):
        return RingGather(
            courier, rows_of(chunk, 0, RB // 2), rows_of(chunk, RB // 2, RB // 2),
            x, x_right, x_left,
        )

    def forward(chunk, pos):
        ref = rows_of(chunk, 0, RB)(pos)
        across[chunk].append(courier.send(ref, ref, partner))

    def multiply(chunk, order):
        low, size = chunks[chunk]
        pos = mod(x + (0, 1, 3, 2)[order], 4)
        across[chunk][order].wait_recv()
        product = lax.dot_general(
            own[:, low:low + size], panel[pos, :, low:low + size],
            (((1,), (1,)), ((), ())), preferred_element_type=f32,
        )
        product = (product * (1.0 / N)).reshape(4, 2, CAP, PIECE_COLS)
        part[pos] = part[pos] + product if chunk else product

    assemble(0)
    ring_0 = ring(0)
    forward(0, x)
    ring_0.relay()
    ring_0.near()
    forward(0, mod(x + 1, 4))
    forward(0, mod(x + 3, 4))
    assemble(1)
    ring_1 = ring(1)
    forward(1, x)
    multiply(0, 0)
    ring_0.far()
    forward(0, mod(x + 2, 4))
    ring_1.relay()
    multiply(0, 1)
    multiply(0, 2)
    multiply(0, 3)
    ring_1.near()
    forward(1, mod(x + 1, 4))
    forward(1, mod(x + 3, 4))
    multiply(1, 0)
    multiply(1, 1)
    multiply(1, 2)
    ring_1.far()
    forward(1, mod(x + 2, 4))
    multiply(1, 3)

    z_right, z_left = device(x, y, mod(z + 1, 4), core), device(x, y, mod(z + 3, 4), core)
    y_right, y_left = device(x, mod(y + 1, 4), z, core), device(x, mod(y + 3, 4), z, core)
    first, second = (lambda r: r.at[0:2]), (lambda r: r.at[2:4])
    upper, lower = (lambda r: r.at[0:32]), (lambda r: r.at[32:CAP])

    def bufs(tmp_a, tmp_b, recv, half):
        return tmp_a.at[half], tmp_b.at[half], recv.at[half, 0], recv.at[half, 1]

    big = lambda half: bufs(big_tmp.at[0], big_tmp.at[1], big_recv, half)
    small = lambda half: bufs(small_tmp_a, small_tmp_b, small_recv, half)
    one = RingReduce(
        courier, lambda p: part.at[0:2, p, 0], lambda p: part.at[2:4, p, 0],
        big(0), (first, second), z, z_right, z_left,
    )
    two = RingReduce(
        courier, lambda p: part.at[p, 0:2, 1], lambda p: part.at[p, 2:4, 1],
        big(1), (first, second), y, y_right, y_left,
    )
    one.relay()
    two.relay()
    one.finish()
    part[:, z, 0] = part[:, z, 0] + big_recv[0, 0] + big_recv[0, 1]
    three = RingReduce(
        courier, lambda p: upper(part.at[p, z, 0]), lambda p: lower(part.at[p, z, 0]),
        small(0), (upper, lower), y, y_right, y_left,
    )
    two.finish()
    part[y, :, 1] = part[y, :, 1] + big_recv[1, 0] + big_recv[1, 1]
    four = RingReduce(
        courier, lambda p: upper(part.at[y, p, 1]), lambda p: lower(part.at[y, p, 1]),
        small(1), (upper, lower), z, z_right, z_left,
    )
    three.relay()
    four.relay()
    three.finish()
    gram_piece[0:CAP] = part[y, z, 0] + small_recv[0, 0] + small_recv[0, 1]
    four.finish()
    gram_piece[CAP:2 * CAP] = part[y, z, 1] + small_recv[1, 0] + small_recv[1, 1]
    courier.drain()
    for chunk in range(2):
        for index, (dy, dz) in enumerate(offsets):
            if dy or dz:
                outward(chunk, index, dy, dz).wait_send()
            else:
                @pl.when(jnp.logical_not(at_home))
                def _():
                    outward(chunk, index, 0, 0).wait_send()


def split(value):
    high = value.astype(bf16)
    return high, (value - high.astype(f32)).astype(bf16)


def update_kernel(
    slot_rows, gram_piece, panel, result, gram_cols, gram_rows, square, poly,
    pick, sums, outgoing, send_sem, recv_sem, out_send, out_recv,
):
    x, y, z, core = position()
    greet(x, y, z, core)
    courier = Courier(send_sem, recv_sem)
    partner = device(x, y, z, 1 - core)
    z_right, z_left = device(x, y, mod(z + 1, 4), core), device(x, y, mod(z + 3, 4), core)
    y_right, y_left = device(x, mod(y + 1, 4), z, core), device(x, mod(y + 3, 4), z, core)
    x_right, x_left = device(mod(x + 1, 4), y, z, core), device(mod(x + 3, 4), y, z, core)

    for h, value in enumerate(split(gram_piece[...])):
        gram_cols[h, x, core, z] = value
        gram_rows[h, y] = value
    upper, lower = (lambda r: r.at[0:64]), (lambda r: r.at[64:PIECE_ROWS])

    def forward(ref):
        return courier.send(ref, ref, partner)

    hi_z = RingGather(
        courier, lambda p: upper(gram_cols.at[0, x, core, p]),
        lambda p: lower(gram_cols.at[0, x, core, p]), z, z_right, z_left,
    )
    lo_x = RingGather(
        courier, lambda p: upper(gram_cols.at[1, p, core, z]),
        lambda p: lower(gram_cols.at[1, p, core, z]), x, x_right, x_left,
    )
    rows_y = RingGather(
        courier, lambda p: gram_rows.at[0, p], lambda p: gram_rows.at[1, p], y, y_right, y_left,
    )
    hi_z.relay()
    lo_x.relay()
    hi_z.near()
    hi_z.far()
    hi_x = RingGather(
        courier, lambda p: gram_cols.at[0, p, core, 0:2],
        lambda p: gram_cols.at[0, p, core, 2:4], x, x_right, x_left,
    )
    across = [forward(gram_cols.at[0, x, core])]
    lo_x.near()
    lo_x.far()
    lo_z = RingGather(
        courier, lambda p: gram_cols.at[1, 0:2, core, p],
        lambda p: gram_cols.at[1, 2:4, core, p], z, z_right, z_left,
    )
    across.append(forward(gram_cols.at[1, :, core, z]))
    rows_y.relay()
    hi_x.relay()
    lo_z.relay()
    rows_y.near()
    rows_y.far()
    hi_x.near()
    for step in (1, 3):
        across.append(forward(gram_cols.at[0, mod(x + step, 4), core]))
    lo_z.near()
    for step in (1, 3):
        across.append(forward(gram_cols.at[1, :, core, mod(z + step, 4)]))

    def square_high(m):
        left = jnp.concatenate([gram_rows[0, m], gram_rows[1, m]], axis=0)
        both = jnp.dot(
            left, gram_cols[0, m].reshape(PIECE_COLS, PIECE_COLS), preferred_element_type=f32
        )
        return both[0:PIECE_ROWS] + both[PIECE_ROWS:]

    across[0].wait_recv()
    square[...] = square_high(x)
    hi_x.far()
    across.append(forward(gram_cols.at[0, mod(x + 2, 4), core]))
    lo_z.far()
    across.append(forward(gram_cols.at[1, :, core, mod(z + 2, 4)]))
    for step, copy in ((1, across[2]), (3, across[3]), (2, across[6])):
        copy.wait_recv()
        square[...] += square_high(mod(x + step, 4))
    for index in (1, 4, 5, 7):
        across[index].wait_recv()

    @pl.loop(0, 4)
    def _(m):
        low = gram_cols[1, m].reshape(PIECE_COLS, PIECE_COLS)
        square[...] += jnp.dot(gram_rows[0, m], low, preferred_element_type=f32)

    for h, value in enumerate(split(cubic_coef * gram_piece[...] + quintic_coef * square[...])):
        poly[h, y, z] = value
    hi_z = RingGather(
        courier, lambda p: upper(poly.at[0, y, p]), lambda p: lower(poly.at[0, y, p]),
        z, z_right, z_left,
    )
    lo_y = RingGather(
        courier, lambda p: upper(poly.at[1, p, z]), lambda p: lower(poly.at[1, p, z]),
        y, y_right, y_left,
    )
    own = panel.at[x, pl.ds(pl.multiple_of(core * RB, RB), RB)]
    sums[...] = linear_coef * own[...].astype(f32)

    def term(h, m, low, size):
        return jnp.dot(
            poly[h, m].reshape(RB, PIECE_COLS), panel[m, :, low:low + size],
            preferred_element_type=f32,
        )

    def add_high(m):
        for low, size in ((0, 640), (640, 512)):
            sums[:, low:low + size] += term(0, m, low, size)

    hi_z.relay()
    lo_y.relay()
    hi_z.near()
    hi_z.far()
    hi_y = RingGather(
        courier, lambda p: poly.at[0, p, 0:2], lambda p: poly.at[0, p, 2:4], y, y_right, y_left,
    )
    lo_y.near()
    lo_y.far()
    lo_z = RingGather(
        courier, lambda p: poly.at[1, 0:2, p], lambda p: poly.at[1, 2:4, p], z, z_right, z_left,
    )
    add_high(y)
    hi_y.relay()
    lo_z.relay()
    hi_y.near()
    add_high(mod(y + 1, 4))
    add_high(mod(y + 3, 4))
    lo_z.near()
    hi_y.far()
    lo_z.far()

    block = y * 4 + z
    at_home = core == mod(y, 2)
    chunks = ((0, 256), (256, 384), (640, 512))
    offsets = [(dh, dz, dc) for dh in (1, 0) for dz in (2, 1, 3, 0) for dc in (1, 0)]

    def place(dh, dz, dc):
        y_to = core + 2 * mod(lax.div(y, jnp.int32(2)) + dh, 2)
        z_to, core_to = mod(z + dz, 4), mod(core + dc, 2)
        return y_to, z_to, core_to

    def window(source, low, size):
        return result.at[:, pl.ds(pl.multiple_of(source * WIDTH + low, 128), size)]

    def outward(chunk, index, offset):
        low, size = chunks[chunk]
        y_to, z_to, core_to = place(*offset)
        return pltpu.make_async_remote_copy(
            src_ref=outgoing.at[index, :, low:low + size],
            dst_ref=window(block, low, size),
            send_sem=out_send.at[chunk, index],
            recv_sem=out_recv.at[chunk, block],
            device_id=device(x, y_to, z_to, core_to),
            device_id_type=MESH,
        )

    row_ids = lax.broadcasted_iota(jnp.int32, (CAP, RB), 1)
    for index, offset in enumerate(offsets):
        y_to, z_to, core_to = place(*offset)
        g = (lax.div(y_to, jnp.int32(2)) * 4 + z_to) * 2 + core_to
        pick[index * CAP:(index + 1) * CAP] = (row_ids == slot_rows[g]).astype(f32)

    for chunk, (low, size) in enumerate(chunks):
        total = sums[:, low:low + size] + term(0, mod(y + 2, 4), low, size)
        for m in range(4):
            total = total + term(1, m, low, size)
        high, rest = split(total)
        moved = jnp.dot(pick[...].astype(bf16), high, preferred_element_type=f32)
        moved = moved + jnp.dot(pick[...].astype(bf16), rest, preferred_element_type=f32)
        outgoing[:, :, low:low + size] = moved.reshape(16, CAP, size)
        for index, offset in enumerate(offsets):
            if any(offset):
                outward(chunk, index, offset).start()
            else:
                @pl.when(at_home)
                def _():
                    pltpu.make_async_copy(
                        outgoing.at[index, :, low:low + size], window(block, low, size),
                        out_recv.at[chunk, block],
                    ).start()

                @pl.when(jnp.logical_not(at_home))
                def _():
                    outward(chunk, index, offset).start()
    for chunk, (low, size) in enumerate(chunks):
        for source in range(16):
            pltpu.make_async_copy(
                window(source, low, size), window(source, low, size), out_recv.at[chunk, source]
            ).wait()
    courier.drain()
    for chunk in range(len(chunks)):
        for index, offset in enumerate(offsets):
            if any(offset):
                outward(chunk, index, offset).wait_send()
            else:
                @pl.when(jnp.logical_not(at_home))
                def _():
                    outward(chunk, index, offset).wait_send()


VMEM_LIMIT = 64000 * 1024
in_vmem = pl.BlockSpec(memory_space=pltpu.VMEM)
anywhere = pl.BlockSpec(memory_space=pl.ANY)


def body(shards, counts):
    x, _, _, core = position()
    row_block = x * 2 + core
    my_counts = lax.dynamic_slice_in_dim(counts, row_block, 1, 0)
    my_starts = jnp.cumsum(my_counts, axis=1) - my_counts
    slots = jnp.arange(CAP, dtype=jnp.int32)[None, :]
    target_rows = jnp.where(
        slots < my_counts[0][:, None], my_starts[0][:, None] + slots, -1
    ).reshape(1, 16 * CAP)

    panel, gram_piece = pl.pallas_call(
        gram_kernel,
        name="gram_kernel",
        out_shape=(
            jax.ShapeDtypeStruct((4, 2 * RB, WIDTH), bf16),
            jax.ShapeDtypeStruct((PIECE_ROWS, PIECE_COLS), f32),
        ),
        in_specs=[anywhere, in_vmem],
        out_specs=(in_vmem, in_vmem),
        scratch_shapes=[
            pltpu.VMEM((16, CAP, WIDTH), bf16),
            pltpu.VMEM((16 * CAP, WIDTH), f32),
            pltpu.VMEM((4, 4, 2, CAP, PIECE_COLS), f32),
            pltpu.VMEM((2, 2, 2, CAP, PIECE_COLS), f32),
            pltpu.VMEM((2, 2, 4, CAP, PIECE_COLS), f32),
            pltpu.VMEM((2, 32, PIECE_COLS), f32),
            pltpu.VMEM((2, CAP - 32, PIECE_COLS), f32),
            pltpu.VMEM((2, 2, CAP, PIECE_COLS), f32),
            pltpu.SemaphoreType.DMA((56,)),
            pltpu.SemaphoreType.DMA((56,)),
            pltpu.SemaphoreType.DMA((2, 16)),
            pltpu.SemaphoreType.DMA((2, 16)),
        ],
        compiler_params=pltpu.CompilerParams(
            collective_id=0, has_side_effects=True, vmem_limit_bytes=VMEM_LIMIT
        ),
    )(shards[0, 0], target_rows)

    result = pl.pallas_call(
        update_kernel,
        name="update_kernel",
        out_shape=jax.ShapeDtypeStruct((CAP, N), f32),
        in_specs=[in_vmem, in_vmem, in_vmem],
        out_specs=anywhere,
        scratch_shapes=[
            pltpu.VMEM((2, 4, 2, 4, PIECE_ROWS, PIECE_COLS), bf16),
            pltpu.VMEM((2, 4, PIECE_ROWS, PIECE_COLS), bf16),
            pltpu.VMEM((PIECE_ROWS, PIECE_COLS), f32),
            pltpu.VMEM((2, 4, 4, PIECE_ROWS, PIECE_COLS), bf16),
            pltpu.VMEM((16 * CAP, RB), f32),
            pltpu.VMEM((RB, WIDTH), f32),
            pltpu.VMEM((16, CAP, WIDTH), f32),
            pltpu.SemaphoreType.DMA((64,)),
            pltpu.SemaphoreType.DMA((64,)),
            pltpu.SemaphoreType.DMA((3, 16)),
            pltpu.SemaphoreType.DMA((3, 16)),
        ],
        compiler_params=pltpu.CompilerParams(
            collective_id=1, has_side_effects=True, vmem_limit_bytes=VMEM_LIMIT
        ),
    )(target_rows.reshape(16, CAP, 1), gram_piece, panel)
    return result.reshape(1, 1, CAP, N)


def solution(mesh):
    placed = (P("gr", "gc", None, None), P())
    return jax.shard_map(
        body, mesh=mesh, in_specs=placed, out_specs=P("gr", "gc", None, None), check_vma=False
    )
```

```python
import jax
import jax.numpy as jnp
from jax import lax
from jax.experimental import pallas as pl
from jax.experimental.pallas import tpu as pltpu
from jax.sharding import PartitionSpec as P

M = 3584
N = 18432
CAP = 56
RB = 448
WIDTH = 1152
PIECE_ROWS = 112
PIECE_COLS = 896

linear_coef = 3.4445
cubic_coef = -4.775
quintic_coef = 2.0315

MESH = pl.DeviceIdType.MESH
f32 = jnp.float32
bf16 = jnp.bfloat16


def mod(value, size):
    return lax.rem(value, jnp.int32(size))


def position():
    gr = lax.axis_index("gr")
    gc = lax.axis_index("gc")
    half = lax.div(gr, jnp.int32(2))
    x = lax.div(gc, jnp.int32(2))
    y = lax.div(half, jnp.int32(4)) * 2 + mod(gc, 2)
    return x, y, mod(half, 4), mod(gr, 2)


def device(x, y, z, core):
    return {
        "gr": (lax.div(y, jnp.int32(2)) * 4 + z) * 2 + core,
        "gc": x * 2 + mod(y, 2),
    }


def greet(x, y, z, core):
    barrier = pltpu.get_barrier_semaphore()
    count = 0
    for dy in range(4):
        for dz in range(4):
            for dc in range(2):
                if dy or dz or dc:
                    target = device(x, mod(y + dy, 4), mod(z + dz, 4), mod(core + dc, 2))
                    pl.semaphore_signal(barrier, inc=1, device_id=target, device_id_type=MESH)
                    count += 1
    for dx in (1, 3):
        target = device(mod(x + dx, 4), y, z, core)
        pl.semaphore_signal(barrier, inc=1, device_id=target, device_id_type=MESH)
        count += 1
    pl.semaphore_wait(barrier, count)


class Courier:
    def __init__(self, send_sem, recv_sem):
        self.send_sem, self.recv_sem = send_sem, recv_sem
        self.copies = []

    def send(self, src, dst, target):
        index = len(self.copies)
        copy = pltpu.make_async_remote_copy(
            src_ref=src,
            dst_ref=dst,
            send_sem=self.send_sem.at[index],
            recv_sem=self.recv_sem.at[index],
            device_id=target,
            device_id_type=MESH,
        )
        self.copies.append(copy)
        copy.start()
        return copy

    def drain(self):
        for copy in self.copies:
            copy.wait_send()


class RingGather:
    def __init__(self, courier, part_a, part_b, pos, right, left):
        self.courier, self.part_a, self.part_b = courier, part_a, part_b
        self.pos, self.right, self.left = pos, right, left
        a, b = part_a(pos), part_b(pos)
        self.a_right = courier.send(a, a, right)
        self.b_left = courier.send(b, b, left)
        self.b_right = courier.send(b, b, right)
        self.a_left = courier.send(a, a, left)

    def relay(self):
        self.a_right.wait_recv()
        a = self.part_a(mod(self.pos + 3, 4))
        self.a_far = self.courier.send(a, a, self.right)
        self.b_left.wait_recv()
        b = self.part_b(mod(self.pos + 1, 4))
        self.b_far = self.courier.send(b, b, self.left)

    def near(self):
        self.b_right.wait_recv()
        self.a_left.wait_recv()

    def far(self):
        self.a_far.wait_recv()
        self.b_far.wait_recv()


class RingReduce:
    def __init__(self, courier, part_a, part_b, bufs, cut, pos, right, left):
        self.courier, self.part_a, self.part_b = courier, part_a, part_b
        self.pos, self.right, self.left = pos, right, left
        self.tmp_a, self.tmp_b, self.from_left, self.from_right = bufs
        self.in_a, self.in_b = cut

    def start_a(self):
        send, pos, part = self.courier.send, self.pos, self.part_a
        self.a1 = send(part(mod(pos + 2, 4)), self.tmp_a, self.right)
        self.b2 = send(part(mod(pos + 3, 4)), self.in_a(self.from_right), self.left)

    def start_b(self):
        send, pos, part = self.courier.send, self.pos, self.part_b
        self.b1 = send(part(mod(pos + 2, 4)), self.tmp_b, self.left)
        self.a2 = send(part(mod(pos + 1, 4)), self.in_b(self.from_left), self.right)

    def start(self):
        self.start_a()
        self.start_b()

    def relay(self):
        self.a1.wait_recv()
        a = self.part_a(mod(self.pos + 1, 4))
        a[...] = a[...] + self.tmp_a[...]
        self.a3 = self.courier.send(a, self.in_a(self.from_left), self.right)
        self.b1.wait_recv()
        b = self.part_b(mod(self.pos + 3, 4))
        b[...] = b[...] + self.tmp_b[...]
        self.b3 = self.courier.send(b, self.in_b(self.from_right), self.left)

    def finish(self):
        for copy in (self.a2, self.b2, self.a3, self.b3):
            copy.wait_recv()


def gram_kernel(
    shard, target_rows, panel, gram_piece, received, wide, part,
    big_tmp, big_recv, small_tmp_a, small_tmp_b, small_recv,
    send_sem, recv_sem, in_send, in_recv,
):
    x, y, z, core = position()
    greet(x, y, z, core)
    y_lo = mod(y, 2)
    me = lax.axis_index("gr")
    at_home = core == y_lo

    chunks = ((0, 512), (512, 640))

    def columns(chunk, dy, dz):
        low, size = chunks[chunk]
        block = mod(y + dy, 4) * 4 + mod(z + dz, 4)
        return shard.at[:, pl.ds(pl.multiple_of(block * WIDTH + low, 128), size)]

    def landing(chunk, source):
        low, size = chunks[chunk]
        return received.at[source, :, low:low + size]

    def outward(chunk, index, dy, dz):
        return pltpu.make_async_remote_copy(
            src_ref=columns(chunk, dy, dz),
            dst_ref=landing(chunk, me),
            send_sem=in_send.at[chunk, index],
            recv_sem=in_recv.at[chunk, me],
            device_id=device(x, mod(y + dy, 4), mod(z + dz, 4), y_lo),
            device_id_type=MESH,
        )

    offsets = [(dy, dz) for dy in range(4) for dz in range(4)]
    offsets = sorted(offsets, key=lambda o: -(min(o[0], 4 - o[0]) + min(o[1], 4 - o[1])))
    for chunk in range(2):
        for index, (dy, dz) in enumerate(offsets):
            if dy or dz:
                outward(chunk, index, dy, dz).start()
            else:
                @pl.when(at_home)
                def _():
                    pltpu.make_async_copy(
                        columns(chunk, 0, 0), landing(chunk, me), in_recv.at[chunk, me]
                    ).start()

                @pl.when(jnp.logical_not(at_home))
                def _():
                    outward(chunk, index, 0, 0).start()

    courier = Courier(send_sem, recv_sem)
    partner = device(x, y, z, 1 - core)
    x_right, x_left = device(mod(x + 1, 4), y, z, core), device(mod(x + 3, 4), y, z, core)
    rows = lax.broadcasted_iota(jnp.int32, (RB, 16 * CAP), 0)
    own = panel.at[x, pl.ds(pl.multiple_of(core * RB, RB), RB)]
    across = [[], []]

    def assemble(chunk):
        low, size = chunks[chunk]
        for g in range(16):
            pltpu.make_async_copy(
                landing(chunk, g), landing(chunk, g), in_recv.at[chunk, g]
            ).wait()
            wide[g * CAP:(g + 1) * CAP, low:low + size] = (
                received[g, :, low:low + size].astype(f32)
            )
        pick = (rows == target_rows[...]).astype(f32).astype(bf16)
        own[:, low:low + size] = jnp.dot(
            pick, wide[:, low:low + size].astype(bf16), preferred_element_type=f32
        ).astype(bf16)

    def rows_of(chunk, first, count):
        low, size = chunks[chunk]

        def part_of(pos):
            start = pl.multiple_of(core * RB + first, 32)
            return panel.at[pos, pl.ds(start, count), low:low + size]
        return part_of

    def ring(chunk):
        return RingGather(
            courier, rows_of(chunk, 0, RB // 2), rows_of(chunk, RB // 2, RB // 2),
            x, x_right, x_left,
        )

    def forward(chunk, pos):
        ref = rows_of(chunk, 0, RB)(pos)
        across[chunk].append(courier.send(ref, ref, partner))

    def multiply(chunk, order):
        low, size = chunks[chunk]
        pos = mod(x + (0, 1, 3, 2)[order], 4)
        across[chunk][order].wait_recv()
        product = lax.dot_general(
            own[:, low:low + size], panel[pos, :, low:low + size],
            (((1,), (1,)), ((), ())), preferred_element_type=f32,
        )
        product = (product * (1.0 / N)).reshape(4, 2, CAP, PIECE_COLS)
        part[order] = part[order] + product if chunk else product

    assemble(0)
    ring_0 = ring(0)
    forward(0, x)
    ring_0.relay()
    ring_0.near()
    forward(0, mod(x + 1, 4))
    forward(0, mod(x + 3, 4))
    assemble(1)
    ring_1 = ring(1)
    forward(1, x)
    multiply(0, 0)
    ring_0.far()
    forward(0, mod(x + 2, 4))
    ring_1.relay()
    multiply(0, 1)
    multiply(0, 2)
    multiply(0, 3)
    ring_1.near()
    forward(1, mod(x + 1, 4))
    forward(1, mod(x + 3, 4))
    z_right, z_left = device(x, y, mod(z + 1, 4), core), device(x, y, mod(z + 3, 4), core)
    y_right, y_left = device(x, mod(y + 1, 4), z, core), device(x, mod(y + 3, 4), z, core)
    first, second = (lambda r: r.at[0:2]), (lambda r: r.at[2:4])
    upper, lower = (lambda r: r.at[0:32]), (lambda r: r.at[32:CAP])

    def bufs(tmp_a, tmp_b, recv, half):
        return tmp_a.at[half], tmp_b.at[half], recv.at[half, 0], recv.at[half, 1]

    big = lambda half: bufs(big_tmp.at[0], big_tmp.at[1], big_recv, half)
    small = lambda half: bufs(small_tmp_a, small_tmp_b, small_recv, half)
    def at(p):
        step = mod(p + 4 - x, 4)
        return step + lax.div(step, jnp.int32(2)) * (5 - 2 * step)

    one = RingReduce(
        courier, lambda p: part.at[0:2, p, 0], lambda p: part.at[2:4, p, 0],
        big(0), (first, second), z, z_right, z_left,
    )
    two = RingReduce(
        courier, lambda p: part.at[at(p), 0:2, 1], lambda p: part.at[at(p), 2:4, 1],
        big(1), (first, second), y, y_right, y_left,
    )
    multiply(1, 0)
    multiply(1, 1)
    one.start_a()
    multiply(1, 2)
    ring_1.far()
    forward(1, mod(x + 2, 4))
    multiply(1, 3)
    one.start_b()
    two.start()
    one.relay()
    two.relay()
    one.finish()
    part[:, z, 0] = part[:, z, 0] + big_recv[0, 0] + big_recv[0, 1]
    three = RingReduce(
        courier, lambda p: upper(part.at[at(p), z, 0]), lambda p: lower(part.at[at(p), z, 0]),
        small(0), (upper, lower), y, y_right, y_left,
    )
    three.start()
    two.finish()
    mine = at(y)
    part[mine, :, 1] = part[mine, :, 1] + big_recv[1, 0] + big_recv[1, 1]
    four = RingReduce(
        courier, lambda p: upper(part.at[mine, p, 1]), lambda p: lower(part.at[mine, p, 1]),
        small(1), (upper, lower), z, z_right, z_left,
    )
    four.start()
    three.relay()
    four.relay()
    three.finish()
    gram_piece[0:CAP] = part[mine, z, 0] + small_recv[0, 0] + small_recv[0, 1]
    four.finish()
    gram_piece[CAP:2 * CAP] = part[mine, z, 1] + small_recv[1, 0] + small_recv[1, 1]
    courier.drain()
    for chunk in range(2):
        for index, (dy, dz) in enumerate(offsets):
            if dy or dz:
                outward(chunk, index, dy, dz).wait_send()
            else:
                @pl.when(jnp.logical_not(at_home))
                def _():
                    outward(chunk, index, 0, 0).wait_send()


def split(value):
    high = value.astype(bf16)
    return high, (value - high.astype(f32)).astype(bf16)


def update_kernel(
    slot_rows, gram_piece, panel, result, gram_cols, gram_rows, square, poly,
    pick, sums, outgoing, send_sem, recv_sem, out_send, out_recv,
):
    x, y, z, core = position()
    greet(x, y, z, core)
    courier = Courier(send_sem, recv_sem)
    partner = device(x, y, z, 1 - core)
    z_right, z_left = device(x, y, mod(z + 1, 4), core), device(x, y, mod(z + 3, 4), core)
    y_right, y_left = device(x, mod(y + 1, 4), z, core), device(x, mod(y + 3, 4), z, core)
    x_right, x_left = device(mod(x + 1, 4), y, z, core), device(mod(x + 3, 4), y, z, core)

    for h, value in enumerate(split(gram_piece[...])):
        gram_cols[h, x, core, z] = value
        gram_rows[h, y] = value
    upper, lower = (lambda r: r.at[0:64]), (lambda r: r.at[64:PIECE_ROWS])

    def forward(ref):
        return courier.send(ref, ref, partner)

    hi_z = RingGather(
        courier, lambda p: upper(gram_cols.at[0, x, core, p]),
        lambda p: lower(gram_cols.at[0, x, core, p]), z, z_right, z_left,
    )
    lo_x = RingGather(
        courier, lambda p: upper(gram_cols.at[1, p, core, z]),
        lambda p: lower(gram_cols.at[1, p, core, z]), x, x_right, x_left,
    )
    rows_y = RingGather(
        courier, lambda p: gram_rows.at[0, p], lambda p: gram_rows.at[1, p], y, y_right, y_left,
    )
    hi_z.relay()
    lo_x.relay()
    hi_z.near()
    hi_z.far()
    hi_x = RingGather(
        courier, lambda p: gram_cols.at[0, p, core, 0:2],
        lambda p: gram_cols.at[0, p, core, 2:4], x, x_right, x_left,
    )
    across = [forward(gram_cols.at[0, x, core])]
    lo_x.near()
    lo_x.far()
    lo_z = RingGather(
        courier, lambda p: gram_cols.at[1, 0:2, core, p],
        lambda p: gram_cols.at[1, 2:4, core, p], z, z_right, z_left,
    )
    across.append(forward(gram_cols.at[1, :, core, z]))
    rows_y.relay()
    hi_x.relay()
    lo_z.relay()
    rows_y.near()
    rows_y.far()
    hi_x.near()
    for step in (1, 3):
        across.append(forward(gram_cols.at[0, mod(x + step, 4), core]))
    lo_z.near()
    for step in (1, 3):
        across.append(forward(gram_cols.at[1, :, core, mod(z + step, 4)]))

    def square_high(m):
        left = jnp.concatenate([gram_rows[0, m], gram_rows[1, m]], axis=0)
        both = jnp.dot(
            left, gram_cols[0, m].reshape(PIECE_COLS, PIECE_COLS), preferred_element_type=f32
        )
        return both[0:PIECE_ROWS] + both[PIECE_ROWS:]

    across[0].wait_recv()
    square[...] = square_high(x)
    hi_x.far()
    across.append(forward(gram_cols.at[0, mod(x + 2, 4), core]))
    lo_z.far()
    across.append(forward(gram_cols.at[1, :, core, mod(z + 2, 4)]))
    for step, copy in ((1, across[2]), (3, across[3]), (2, across[6])):
        copy.wait_recv()
        square[...] += square_high(mod(x + step, 4))
    for index in (1, 4, 5, 7):
        across[index].wait_recv()

    @pl.loop(0, 4)
    def _(m):
        low = gram_cols[1, m].reshape(PIECE_COLS, PIECE_COLS)
        square[...] += jnp.dot(gram_rows[0, m], low, preferred_element_type=f32)

    for h, value in enumerate(split(cubic_coef * gram_piece[...] + quintic_coef * square[...])):
        poly[h, y, z] = value
    hi_z = RingGather(
        courier, lambda p: upper(poly.at[0, y, p]), lambda p: lower(poly.at[0, y, p]),
        z, z_right, z_left,
    )
    lo_y = RingGather(
        courier, lambda p: upper(poly.at[1, p, z]), lambda p: lower(poly.at[1, p, z]),
        y, y_right, y_left,
    )
    own = panel.at[x, pl.ds(pl.multiple_of(core * RB, RB), RB)]
    sums[...] = linear_coef * own[...].astype(f32)

    def term(h, m, low, size):
        return jnp.dot(
            poly[h, m].reshape(RB, PIECE_COLS), panel[m, :, low:low + size],
            preferred_element_type=f32,
        )

    def add_high(m):
        for low, size in ((0, 640), (640, 512)):
            sums[:, low:low + size] += term(0, m, low, size)

    hi_z.relay()
    lo_y.relay()
    hi_z.near()
    hi_z.far()
    hi_y = RingGather(
        courier, lambda p: poly.at[0, p, 0:2], lambda p: poly.at[0, p, 2:4], y, y_right, y_left,
    )
    lo_y.near()
    lo_y.far()
    lo_z = RingGather(
        courier, lambda p: poly.at[1, 0:2, p], lambda p: poly.at[1, 2:4, p], z, z_right, z_left,
    )
    add_high(y)
    hi_y.relay()
    lo_z.relay()
    hi_y.near()
    add_high(mod(y + 1, 4))
    add_high(mod(y + 3, 4))
    lo_z.near()
    hi_y.far()
    lo_z.far()

    block = y * 4 + z
    at_home = core == mod(y, 2)
    chunks = ((0, 256), (256, 384), (640, 512))
    offsets = [(dh, dz, dc) for dh in (1, 0) for dz in (2, 1, 3, 0) for dc in (1, 0)]

    def place(dh, dz, dc):
        y_to = core + 2 * mod(lax.div(y, jnp.int32(2)) + dh, 2)
        z_to, core_to = mod(z + dz, 4), mod(core + dc, 2)
        return y_to, z_to, core_to

    def window(source, low, size):
        return result.at[:, pl.ds(pl.multiple_of(source * WIDTH + low, 128), size)]

    def outward(chunk, index, offset):
        low, size = chunks[chunk]
        y_to, z_to, core_to = place(*offset)
        return pltpu.make_async_remote_copy(
            src_ref=outgoing.at[index, :, low:low + size],
            dst_ref=window(block, low, size),
            send_sem=out_send.at[chunk, index],
            recv_sem=out_recv.at[chunk, block],
            device_id=device(x, y_to, z_to, core_to),
            device_id_type=MESH,
        )

    row_ids = lax.broadcasted_iota(jnp.int32, (CAP, RB), 1)
    for index, offset in enumerate(offsets):
        y_to, z_to, core_to = place(*offset)
        g = (lax.div(y_to, jnp.int32(2)) * 4 + z_to) * 2 + core_to
        pick[index * CAP:(index + 1) * CAP] = (row_ids == slot_rows[g]).astype(f32)

    for chunk, (low, size) in enumerate(chunks):
        total = sums[:, low:low + size] + term(0, mod(y + 2, 4), low, size)
        for m in range(4):
            total = total + term(1, m, low, size)
        high, rest = split(total)
        moved = jnp.dot(pick[...].astype(bf16), high, preferred_element_type=f32)
        moved = moved + jnp.dot(pick[...].astype(bf16), rest, preferred_element_type=f32)
        outgoing[:, :, low:low + size] = moved.reshape(16, CAP, size)
        for index, offset in enumerate(offsets):
            if any(offset):
                outward(chunk, index, offset).start()
            else:
                @pl.when(at_home)
                def _():
                    pltpu.make_async_copy(
                        outgoing.at[index, :, low:low + size], window(block, low, size),
                        out_recv.at[chunk, block],
                    ).start()

                @pl.when(jnp.logical_not(at_home))
                def _():
                    outward(chunk, index, offset).start()
    for chunk, (low, size) in enumerate(chunks):
        for source in range(16):
            pltpu.make_async_copy(
                window(source, low, size), window(source, low, size), out_recv.at[chunk, source]
            ).wait()
    courier.drain()
    for chunk in range(len(chunks)):
        for index, offset in enumerate(offsets):
            if any(offset):
                outward(chunk, index, offset).wait_send()
            else:
                @pl.when(jnp.logical_not(at_home))
                def _():
                    outward(chunk, index, offset).wait_send()


VMEM_LIMIT = 64000 * 1024
in_vmem = pl.BlockSpec(memory_space=pltpu.VMEM)
anywhere = pl.BlockSpec(memory_space=pl.ANY)


def body(shards, counts):
    x, _, _, core = position()
    row_block = x * 2 + core
    my_counts = lax.dynamic_slice_in_dim(counts, row_block, 1, 0)
    my_starts = jnp.cumsum(my_counts, axis=1) - my_counts
    slots = jnp.arange(CAP, dtype=jnp.int32)[None, :]
    target_rows = jnp.where(
        slots < my_counts[0][:, None], my_starts[0][:, None] + slots, -1
    ).reshape(1, 16 * CAP)

    panel, gram_piece = pl.pallas_call(
        gram_kernel,
        name="gram_kernel",
        out_shape=(
            jax.ShapeDtypeStruct((4, 2 * RB, WIDTH), bf16),
            jax.ShapeDtypeStruct((PIECE_ROWS, PIECE_COLS), f32),
        ),
        in_specs=[anywhere, in_vmem],
        out_specs=(in_vmem, in_vmem),
        scratch_shapes=[
            pltpu.VMEM((16, CAP, WIDTH), bf16),
            pltpu.VMEM((16 * CAP, WIDTH), f32),
            pltpu.VMEM((4, 4, 2, CAP, PIECE_COLS), f32),
            pltpu.VMEM((2, 2, 2, CAP, PIECE_COLS), f32),
            pltpu.VMEM((2, 2, 4, CAP, PIECE_COLS), f32),
            pltpu.VMEM((2, 32, PIECE_COLS), f32),
            pltpu.VMEM((2, CAP - 32, PIECE_COLS), f32),
            pltpu.VMEM((2, 2, CAP, PIECE_COLS), f32),
            pltpu.SemaphoreType.DMA((56,)),
            pltpu.SemaphoreType.DMA((56,)),
            pltpu.SemaphoreType.DMA((2, 16)),
            pltpu.SemaphoreType.DMA((2, 16)),
        ],
        compiler_params=pltpu.CompilerParams(
            collective_id=0, has_side_effects=True, vmem_limit_bytes=VMEM_LIMIT
        ),
    )(shards[0, 0], target_rows)

    result = pl.pallas_call(
        update_kernel,
        name="update_kernel",
        out_shape=jax.ShapeDtypeStruct((CAP, N), f32),
        in_specs=[in_vmem, in_vmem, in_vmem],
        out_specs=anywhere,
        scratch_shapes=[
            pltpu.VMEM((2, 4, 2, 4, PIECE_ROWS, PIECE_COLS), bf16),
            pltpu.VMEM((2, 4, PIECE_ROWS, PIECE_COLS), bf16),
            pltpu.VMEM((PIECE_ROWS, PIECE_COLS), f32),
            pltpu.VMEM((2, 4, 4, PIECE_ROWS, PIECE_COLS), bf16),
            pltpu.VMEM((16 * CAP, RB), f32),
            pltpu.VMEM((RB, WIDTH), f32),
            pltpu.VMEM((16, CAP, WIDTH), f32),
            pltpu.SemaphoreType.DMA((64,)),
            pltpu.SemaphoreType.DMA((64,)),
            pltpu.SemaphoreType.DMA((3, 16)),
            pltpu.SemaphoreType.DMA((3, 16)),
        ],
        compiler_params=pltpu.CompilerParams(
            collective_id=1, has_side_effects=True, vmem_limit_bytes=VMEM_LIMIT
        ),
    )(target_rows.reshape(16, CAP, 1), gram_piece, panel)
    return result.reshape(1, 1, CAP, N)


def solution(mesh):
    placed = (P("gr", "gc", None, None), P())
    return jax.shard_map(
        body, mesh=mesh, in_specs=placed, out_specs=P("gr", "gc", None, None), check_vma=False
    )
```

```python
import jax
import jax.numpy as jnp
from jax import lax
from jax.experimental import pallas as pl
from jax.experimental.pallas import tpu as pltpu
from jax.sharding import PartitionSpec as P

M = 3584
N = 18432
CAP = 56
RB = 448
WIDTH = 1152
PIECE_ROWS = 112
PIECE_COLS = 896

linear_coef = 3.4445
cubic_coef = -4.775
quintic_coef = 2.0315

MESH = pl.DeviceIdType.MESH
f32 = jnp.float32
bf16 = jnp.bfloat16


def mod(value, size):
    return lax.rem(value, jnp.int32(size))


def position():
    gr = lax.axis_index("gr")
    gc = lax.axis_index("gc")
    half = lax.div(gr, jnp.int32(2))
    x = lax.div(gc, jnp.int32(2))
    y = lax.div(half, jnp.int32(4)) * 2 + mod(gc, 2)
    return x, y, mod(half, 4), mod(gr, 2)


def device(x, y, z, core):
    return {
        "gr": (lax.div(y, jnp.int32(2)) * 4 + z) * 2 + core,
        "gc": x * 2 + mod(y, 2),
    }


def greet(x, y, z, core):
    barrier = pltpu.get_barrier_semaphore()
    count = 0
    for dy in range(4):
        for dz in range(4):
            for dc in range(2):
                if dy or dz or dc:
                    target = device(x, mod(y + dy, 4), mod(z + dz, 4), mod(core + dc, 2))
                    pl.semaphore_signal(barrier, inc=1, device_id=target, device_id_type=MESH)
                    count += 1
    for dx in (1, 3):
        target = device(mod(x + dx, 4), y, z, core)
        pl.semaphore_signal(barrier, inc=1, device_id=target, device_id_type=MESH)
        count += 1
    pl.semaphore_wait(barrier, count)


class Courier:
    def __init__(self, send_sem, recv_sem):
        self.send_sem, self.recv_sem = send_sem, recv_sem
        self.copies = []

    def send(self, src, dst, target):
        index = len(self.copies)
        copy = pltpu.make_async_remote_copy(
            src_ref=src,
            dst_ref=dst,
            send_sem=self.send_sem.at[index],
            recv_sem=self.recv_sem.at[index],
            device_id=target,
            device_id_type=MESH,
        )
        self.copies.append(copy)
        copy.start()
        return copy

    def drain(self):
        for copy in self.copies:
            copy.wait_send()


class RingGather:
    def __init__(self, courier, part_a, part_b, pos, right, left):
        self.courier, self.part_a, self.part_b = courier, part_a, part_b
        self.pos, self.right, self.left = pos, right, left
        a, b = part_a(pos), part_b(pos)
        self.a_right = courier.send(a, a, right)
        self.b_left = courier.send(b, b, left)
        self.b_right = courier.send(b, b, right)
        self.a_left = courier.send(a, a, left)

    def relay(self):
        self.a_right.wait_recv()
        a = self.part_a(mod(self.pos + 3, 4))
        self.a_far = self.courier.send(a, a, self.right)
        self.b_left.wait_recv()
        b = self.part_b(mod(self.pos + 1, 4))
        self.b_far = self.courier.send(b, b, self.left)

    def near(self):
        self.b_right.wait_recv()
        self.a_left.wait_recv()

    def far(self):
        self.a_far.wait_recv()
        self.b_far.wait_recv()


class RingReduce:
    def __init__(self, courier, part_a, part_b, bufs, cut, pos, right, left):
        self.courier, self.part_a, self.part_b = courier, part_a, part_b
        self.pos, self.right, self.left = pos, right, left
        self.tmp_a, self.tmp_b, self.from_left, self.from_right = bufs
        self.in_a, self.in_b = cut
        far = mod(pos + 2, 4)
        self.a1 = courier.send(part_a(far), self.tmp_a, right)
        self.b1 = courier.send(part_b(far), self.tmp_b, left)
        self.a2 = courier.send(part_b(mod(pos + 1, 4)), self.in_b(self.from_left), right)
        self.b2 = courier.send(part_a(mod(pos + 3, 4)), self.in_a(self.from_right), left)

    def relay(self):
        self.a1.wait_recv()
        a = self.part_a(mod(self.pos + 1, 4))
        a[...] = a[...] + self.tmp_a[...]
        self.a3 = self.courier.send(a, self.in_a(self.from_left), self.right)
        self.b1.wait_recv()
        b = self.part_b(mod(self.pos + 3, 4))
        b[...] = b[...] + self.tmp_b[...]
        self.b3 = self.courier.send(b, self.in_b(self.from_right), self.left)

    def finish(self):
        for copy in (self.a2, self.b2, self.a3, self.b3):
            copy.wait_recv()


def gram_kernel(
    shard, target_rows, panel, gram_piece, received, wide, part,
    big_tmp, big_recv, small_tmp_a, small_tmp_b, small_recv,
    send_sem, recv_sem, in_send, in_recv,
):
    x, y, z, core = position()
    greet(x, y, z, core)
    y_lo = mod(y, 2)
    me = lax.axis_index("gr")
    at_home = core == y_lo

    chunks = ((0, 384), (384, 768))

    def columns(chunk, dy, dz):
        low, size = chunks[chunk]
        block = mod(y + dy, 4) * 4 + mod(z + dz, 4)
        return shard.at[:, pl.ds(pl.multiple_of(block * WIDTH + low, 128), size)]

    def landing(chunk, source):
        low, size = chunks[chunk]
        return received.at[source, :, low:low + size]

    def outward(chunk, index, dy, dz):
        return pltpu.make_async_remote_copy(
            src_ref=columns(chunk, dy, dz),
            dst_ref=landing(chunk, me),
            send_sem=in_send.at[chunk, index],
            recv_sem=in_recv.at[chunk, me],
            device_id=device(x, mod(y + dy, 4), mod(z + dz, 4), y_lo),
            device_id_type=MESH,
        )

    offsets = [(dy, dz) for dy in range(4) for dz in range(4)]
    offsets = sorted(offsets, key=lambda o: -(min(o[0], 4 - o[0]) + min(o[1], 4 - o[1])))
    for chunk in range(2):
        for index, (dy, dz) in enumerate(offsets):
            if dy or dz:
                outward(chunk, index, dy, dz).start()
            else:
                @pl.when(at_home)
                def _():
                    pltpu.make_async_copy(
                        columns(chunk, 0, 0), landing(chunk, me), in_recv.at[chunk, me]
                    ).start()

                @pl.when(jnp.logical_not(at_home))
                def _():
                    outward(chunk, index, 0, 0).start()

    courier = Courier(send_sem, recv_sem)
    partner = device(x, y, z, 1 - core)
    x_right, x_left = device(mod(x + 1, 4), y, z, core), device(mod(x + 3, 4), y, z, core)
    rows = lax.broadcasted_iota(jnp.int32, (RB, 16 * CAP), 0)
    own = panel.at[x, pl.ds(pl.multiple_of(core * RB, RB), RB)]
    across = [[], []]

    def assemble(chunk):
        low, size = chunks[chunk]
        for g in range(16):
            pltpu.make_async_copy(
                landing(chunk, g), landing(chunk, g), in_recv.at[chunk, g]
            ).wait()
            wide[g * CAP:(g + 1) * CAP, low:low + size] = (
                received[g, :, low:low + size].astype(f32)
            )
        pick = (rows == target_rows[...]).astype(f32).astype(bf16)
        own[:, low:low + size] = jnp.dot(
            pick, wide[:, low:low + size].astype(bf16), preferred_element_type=f32
        ).astype(bf16)

    def rows_of(chunk, first, count):
        low, size = chunks[chunk]

        def part_of(pos):
            start = pl.multiple_of(core * RB + first, 32)
            return panel.at[pos, pl.ds(start, count), low:low + size]
        return part_of

    def ring(chunk):
        return RingGather(
            courier, rows_of(chunk, 0, RB // 2), rows_of(chunk, RB // 2, RB // 2),
            x, x_right, x_left,
        )

    def forward(chunk, pos):
        ref = rows_of(chunk, 0, RB)(pos)
        across[chunk].append(courier.send(ref, ref, partner))

    def multiply(chunk, order):
        low, size = chunks[chunk]
        pos = mod(x + (0, 1, 3, 2)[order], 4)
        across[chunk][order].wait_recv()
        product = lax.dot_general(
            own[:, low:low + size], panel[pos, :, low:low + size],
            (((1,), (1,)), ((), ())), preferred_element_type=f32,
        )
        product = (product * (1.0 / N)).reshape(4, 2, CAP, PIECE_COLS)
        part[pos] = part[pos] + product if chunk else product

    assemble(0)
    ring_0 = ring(0)
    forward(0, x)
    ring_0.relay()
    ring_0.near()
    forward(0, mod(x + 1, 4))
    forward(0, mod(x + 3, 4))
    assemble(1)
    ring_1 = ring(1)
    forward(1, x)
    multiply(0, 0)
    ring_0.far()
    forward(0, mod(x + 2, 4))
    ring_1.relay()
    multiply(0, 1)
    multiply(0, 2)
    multiply(0, 3)
    ring_1.near()
    forward(1, mod(x + 1, 4))
    forward(1, mod(x + 3, 4))
    multiply(1, 0)
    multiply(1, 1)
    multiply(1, 2)
    ring_1.far()
    forward(1, mod(x + 2, 4))
    multiply(1, 3)

    z_right, z_left = device(x, y, mod(z + 1, 4), core), device(x, y, mod(z + 3, 4), core)
    y_right, y_left = device(x, mod(y + 1, 4), z, core), device(x, mod(y + 3, 4), z, core)
    first, second = (lambda r: r.at[0:2]), (lambda r: r.at[2:4])
    upper, lower = (lambda r: r.at[0:32]), (lambda r: r.at[32:CAP])

    def bufs(tmp_a, tmp_b, recv, half):
        return tmp_a.at[half], tmp_b.at[half], recv.at[half, 0], recv.at[half, 1]

    big = lambda half: bufs(big_tmp.at[0], big_tmp.at[1], big_recv, half)
    small = lambda half: bufs(small_tmp_a, small_tmp_b, small_recv, half)
    one = RingReduce(
        courier, lambda p: part.at[0:2, p, 0], lambda p: part.at[2:4, p, 0],
        big(0), (first, second), z, z_right, z_left,
    )
    two = RingReduce(
        courier, lambda p: part.at[p, 0:2, 1], lambda p: part.at[p, 2:4, 1],
        big(1), (first, second), y, y_right, y_left,
    )
    one.relay()
    two.relay()
    one.finish()
    part[:, z, 0] = part[:, z, 0] + big_recv[0, 0] + big_recv[0, 1]
    three = RingReduce(
        courier, lambda p: upper(part.at[p, z, 0]), lambda p: lower(part.at[p, z, 0]),
        small(0), (upper, lower), y, y_right, y_left,
    )
    two.finish()
    part[y, :, 1] = part[y, :, 1] + big_recv[1, 0] + big_recv[1, 1]
    four = RingReduce(
        courier, lambda p: upper(part.at[y, p, 1]), lambda p: lower(part.at[y, p, 1]),
        small(1), (upper, lower), z, z_right, z_left,
    )
    three.relay()
    four.relay()
    three.finish()
    gram_piece[0:CAP] = part[y, z, 0] + small_recv[0, 0] + small_recv[0, 1]
    four.finish()
    gram_piece[CAP:2 * CAP] = part[y, z, 1] + small_recv[1, 0] + small_recv[1, 1]
    courier.drain()
    for chunk in range(2):
        for index, (dy, dz) in enumerate(offsets):
            if dy or dz:
                outward(chunk, index, dy, dz).wait_send()
            else:
                @pl.when(jnp.logical_not(at_home))
                def _():
                    outward(chunk, index, 0, 0).wait_send()


def split(value):
    high = value.astype(bf16)
    return high, (value - high.astype(f32)).astype(bf16)


def update_kernel(
    slot_rows, gram_piece, panel, result, gram_cols, gram_rows, square, poly,
    pick, sums, outgoing, send_sem, recv_sem, out_send, out_recv,
):
    x, y, z, core = position()
    greet(x, y, z, core)
    courier = Courier(send_sem, recv_sem)
    partner = device(x, y, z, 1 - core)
    z_right, z_left = device(x, y, mod(z + 1, 4), core), device(x, y, mod(z + 3, 4), core)
    y_right, y_left = device(x, mod(y + 1, 4), z, core), device(x, mod(y + 3, 4), z, core)
    x_right, x_left = device(mod(x + 1, 4), y, z, core), device(mod(x + 3, 4), y, z, core)

    for h, value in enumerate(split(gram_piece[...])):
        gram_cols[h, x, core, z] = value
        gram_rows[h, y] = value
    upper, lower = (lambda r: r.at[0:64]), (lambda r: r.at[64:PIECE_ROWS])

    def forward(ref):
        return courier.send(ref, ref, partner)

    hi_z = RingGather(
        courier, lambda p: upper(gram_cols.at[0, x, core, p]),
        lambda p: lower(gram_cols.at[0, x, core, p]), z, z_right, z_left,
    )
    lo_x = RingGather(
        courier, lambda p: upper(gram_cols.at[1, p, core, z]),
        lambda p: lower(gram_cols.at[1, p, core, z]), x, x_right, x_left,
    )
    rows_y = RingGather(
        courier, lambda p: gram_rows.at[0, p], lambda p: gram_rows.at[1, p], y, y_right, y_left,
    )
    hi_z.relay()
    lo_x.relay()
    hi_z.near()
    hi_z.far()
    hi_x = RingGather(
        courier, lambda p: gram_cols.at[0, p, core, 0:2],
        lambda p: gram_cols.at[0, p, core, 2:4], x, x_right, x_left,
    )
    across = [forward(gram_cols.at[0, x, core])]
    lo_x.near()
    lo_x.far()
    lo_z = RingGather(
        courier, lambda p: gram_cols.at[1, 0:2, core, p],
        lambda p: gram_cols.at[1, 2:4, core, p], z, z_right, z_left,
    )
    across.append(forward(gram_cols.at[1, :, core, z]))
    rows_y.relay()
    hi_x.relay()
    lo_z.relay()
    rows_y.near()
    rows_y.far()
    hi_x.near()
    for step in (1, 3):
        across.append(forward(gram_cols.at[0, mod(x + step, 4), core]))
    lo_z.near()
    for step in (1, 3):
        across.append(forward(gram_cols.at[1, :, core, mod(z + step, 4)]))

    def square_high(m):
        left = jnp.concatenate([gram_rows[0, m], gram_rows[1, m]], axis=0)
        both = jnp.dot(
            left, gram_cols[0, m].reshape(PIECE_COLS, PIECE_COLS), preferred_element_type=f32
        )
        return both[0:PIECE_ROWS] + both[PIECE_ROWS:]

    across[0].wait_recv()
    square[...] = square_high(x)
    hi_x.far()
    across.append(forward(gram_cols.at[0, mod(x + 2, 4), core]))
    lo_z.far()
    across.append(forward(gram_cols.at[1, :, core, mod(z + 2, 4)]))
    for step, copy in ((1, across[2]), (3, across[3]), (2, across[6])):
        copy.wait_recv()
        square[...] += square_high(mod(x + step, 4))
    for index in (1, 4, 5, 7):
        across[index].wait_recv()

    @pl.loop(0, 4)
    def _(m):
        low = gram_cols[1, m].reshape(PIECE_COLS, PIECE_COLS)
        square[...] += jnp.dot(gram_rows[0, m], low, preferred_element_type=f32)

    for h, value in enumerate(split(cubic_coef * gram_piece[...] + quintic_coef * square[...])):
        poly[h, y, z] = value
    hi_z = RingGather(
        courier, lambda p: upper(poly.at[0, y, p]), lambda p: lower(poly.at[0, y, p]),
        z, z_right, z_left,
    )
    lo_y = RingGather(
        courier, lambda p: upper(poly.at[1, p, z]), lambda p: lower(poly.at[1, p, z]),
        y, y_right, y_left,
    )
    own = panel.at[x, pl.ds(pl.multiple_of(core * RB, RB), RB)]
    sums[...] = linear_coef * own[...].astype(f32)

    def term(h, m, low, size):
        return jnp.dot(
            poly[h, m].reshape(RB, PIECE_COLS), panel[m, :, low:low + size],
            preferred_element_type=f32,
        )

    def add_high(m):
        for low, size in ((0, 640), (640, 512)):
            sums[:, low:low + size] += term(0, m, low, size)

    hi_z.relay()
    lo_y.relay()
    hi_z.near()
    hi_z.far()
    hi_y = RingGather(
        courier, lambda p: poly.at[0, p, 0:2], lambda p: poly.at[0, p, 2:4], y, y_right, y_left,
    )
    lo_y.near()
    lo_y.far()
    lo_z = RingGather(
        courier, lambda p: poly.at[1, 0:2, p], lambda p: poly.at[1, 2:4, p], z, z_right, z_left,
    )
    add_high(y)
    hi_y.relay()
    lo_z.relay()
    hi_y.near()
    add_high(mod(y + 1, 4))
    add_high(mod(y + 3, 4))
    lo_z.near()
    hi_y.far()
    lo_z.far()

    block = y * 4 + z
    at_home = core == mod(y, 2)
    chunks = ((0, 256), (256, 384), (640, 512))
    offsets = [(dh, dz, dc) for dh in (1, 0) for dz in (2, 1, 3, 0) for dc in (1, 0)]

    def place(dh, dz, dc):
        y_to = core + 2 * mod(lax.div(y, jnp.int32(2)) + dh, 2)
        z_to, core_to = mod(z + dz, 4), mod(core + dc, 2)
        return y_to, z_to, core_to

    def window(source, low, size):
        return result.at[:, pl.ds(pl.multiple_of(source * WIDTH + low, 128), size)]

    def outward(chunk, index, offset):
        low, size = chunks[chunk]
        y_to, z_to, core_to = place(*offset)
        return pltpu.make_async_remote_copy(
            src_ref=outgoing.at[index, :, low:low + size],
            dst_ref=window(block, low, size),
            send_sem=out_send.at[chunk, index],
            recv_sem=out_recv.at[chunk, block],
            device_id=device(x, y_to, z_to, core_to),
            device_id_type=MESH,
        )

    row_ids = lax.broadcasted_iota(jnp.int32, (CAP, RB), 1)
    for index, offset in enumerate(offsets):
        y_to, z_to, core_to = place(*offset)
        g = (lax.div(y_to, jnp.int32(2)) * 4 + z_to) * 2 + core_to
        pick[index * CAP:(index + 1) * CAP] = (row_ids == slot_rows[g]).astype(f32)

    for chunk, (low, size) in enumerate(chunks):
        total = sums[:, low:low + size] + term(0, mod(y + 2, 4), low, size)
        for m in range(4):
            total = total + term(1, m, low, size)
        high, rest = split(total)
        moved = jnp.dot(pick[...].astype(bf16), high, preferred_element_type=f32)
        moved = moved + jnp.dot(pick[...].astype(bf16), rest, preferred_element_type=f32)
        outgoing[:, :, low:low + size] = moved.reshape(16, CAP, size)
        for index, offset in enumerate(offsets):
            if any(offset):
                outward(chunk, index, offset).start()
            else:
                @pl.when(at_home)
                def _():
                    pltpu.make_async_copy(
                        outgoing.at[index, :, low:low + size], window(block, low, size),
                        out_recv.at[chunk, block],
                    ).start()

                @pl.when(jnp.logical_not(at_home))
                def _():
                    outward(chunk, index, offset).start()
    for chunk, (low, size) in enumerate(chunks):
        for source in range(16):
            pltpu.make_async_copy(
                window(source, low, size), window(source, low, size), out_recv.at[chunk, source]
            ).wait()
    courier.drain()
    for chunk in range(len(chunks)):
        for index, offset in enumerate(offsets):
            if any(offset):
                outward(chunk, index, offset).wait_send()
            else:
                @pl.when(jnp.logical_not(at_home))
                def _():
                    outward(chunk, index, offset).wait_send()


VMEM_LIMIT = 64000 * 1024
in_vmem = pl.BlockSpec(memory_space=pltpu.VMEM)
anywhere = pl.BlockSpec(memory_space=pl.ANY)


def body(shards, counts):
    x, _, _, core = position()
    row_block = x * 2 + core
    my_counts = lax.dynamic_slice_in_dim(counts, row_block, 1, 0)
    my_starts = jnp.cumsum(my_counts, axis=1) - my_counts
    slots = jnp.arange(CAP, dtype=jnp.int32)[None, :]
    target_rows = jnp.where(
        slots < my_counts[0][:, None], my_starts[0][:, None] + slots, -1
    ).reshape(1, 16 * CAP)

    panel, gram_piece = pl.pallas_call(
        gram_kernel,
        name="gram_kernel",
        out_shape=(
            jax.ShapeDtypeStruct((4, 2 * RB, WIDTH), bf16),
            jax.ShapeDtypeStruct((PIECE_ROWS, PIECE_COLS), f32),
        ),
        in_specs=[anywhere, in_vmem],
        out_specs=(in_vmem, in_vmem),
        scratch_shapes=[
            pltpu.VMEM((16, CAP, WIDTH), bf16),
            pltpu.VMEM((16 * CAP, WIDTH), f32),
            pltpu.VMEM((4, 4, 2, CAP, PIECE_COLS), f32),
            pltpu.VMEM((2, 2, 2, CAP, PIECE_COLS), f32),
            pltpu.VMEM((2, 2, 4, CAP, PIECE_COLS), f32),
            pltpu.VMEM((2, 32, PIECE_COLS), f32),
            pltpu.VMEM((2, CAP - 32, PIECE_COLS), f32),
            pltpu.VMEM((2, 2, CAP, PIECE_COLS), f32),
            pltpu.SemaphoreType.DMA((56,)),
            pltpu.SemaphoreType.DMA((56,)),
            pltpu.SemaphoreType.DMA((2, 16)),
            pltpu.SemaphoreType.DMA((2, 16)),
        ],
        compiler_params=pltpu.CompilerParams(
            collective_id=0, has_side_effects=True, vmem_limit_bytes=VMEM_LIMIT
        ),
    )(shards[0, 0], target_rows)

    result = pl.pallas_call(
        update_kernel,
        name="update_kernel",
        out_shape=jax.ShapeDtypeStruct((CAP, N), f32),
        in_specs=[in_vmem, in_vmem, in_vmem],
        out_specs=anywhere,
        scratch_shapes=[
            pltpu.VMEM((2, 4, 2, 4, PIECE_ROWS, PIECE_COLS), bf16),
            pltpu.VMEM((2, 4, PIECE_ROWS, PIECE_COLS), bf16),
            pltpu.VMEM((PIECE_ROWS, PIECE_COLS), f32),
            pltpu.VMEM((2, 4, 4, PIECE_ROWS, PIECE_COLS), bf16),
            pltpu.VMEM((16 * CAP, RB), f32),
            pltpu.VMEM((RB, WIDTH), f32),
            pltpu.VMEM((16, CAP, WIDTH), f32),
            pltpu.SemaphoreType.DMA((64,)),
            pltpu.SemaphoreType.DMA((64,)),
            pltpu.SemaphoreType.DMA((3, 16)),
            pltpu.SemaphoreType.DMA((3, 16)),
        ],
        compiler_params=pltpu.CompilerParams(
            collective_id=1, has_side_effects=True, vmem_limit_bytes=VMEM_LIMIT
        ),
    )(target_rows.reshape(16, CAP, 1), gram_piece, panel)
    return result.reshape(1, 1, CAP, N)


def solution(mesh):
    placed = (P("gr", "gc", None, None), P())
    return jax.shard_map(
        body, mesh=mesh, in_specs=placed, out_specs=P("gr", "gc", None, None), check_vma=False
    )
```
